512 devices in a mesh: rep: 64 (over y, x, core), ch: 8 (over z).
Axes of the slice: x: 4, y: 8, z: 8, core: 2. Of those that a mesh axis runs over, the one named last changes fastest.
Arguments:
- inputs: float32 [128, 14, 14, 512], P('rep'), may hold values from -6 to 6
- grad_out: float32 [128, 14, 14, 1024], P('rep', None, None, 'ch'), may hold values from -81 to 81
- weight: float32 [1024, 3, 3, 512], P('ch'), may hold values from -0.09375 to 0.09375
- momentum: float32 [1024, 3, 3, 512], P(('ch', 'rep')), may hold values from -6 to 6
Outputs:
- input_grad: float32 [128, 14, 14, 512], P('rep', None, None, 'ch')
- new_weight: float32 [1024, 3, 3, 512], P(('ch', 'rep'))
- new_momentum: float32 [1024, 3, 3, 512], P(('ch', 'rep'))
The draws below stay inside these ranges and needn't reach their ends.
All inputs are finite; a program needn't handle non-finite values.
Results may differ from the reference program's by a relative error of at most 0.0001.
Values sent between devices are 32-bit elements; how exact they have to be, the bound alone decides.
No kernel may reach another device: no remote copies, remote signals or barrier semaphores. Data moves between devices by JAX's collectives and lax.ppermute only.
A program may use at most 64 MiB of HBM per device.

```python
import math
import jax
import jax.numpy as jnp
from jax import lax

IMG_DEV = 2
CO = 1024
CI = 512
HH = 14
WW = 14
BATCH = 128
N_REP = 64
N_CH = 8


def draw_inputs(key, part):
    noise_key = jax.random.fold_in(key, 21)
    pattern_key = jax.random.fold_in(key, 22)
    pattern = jnp.clip(jax.random.normal(pattern_key, (HH, WW, CI), jnp.float32), -4.0, 4.0)
    noise = jnp.clip(jax.random.normal(noise_key, (BATCH, HH, WW, CI), jnp.float32), -4.0, 4.0)
    return noise + 0.5 * pattern[None]


def draw_grad_out(key, part):
    jitter_key = jax.random.fold_in(key, 11)
    channel_key = jax.random.fold_in(key, 12)
    common_key = jax.random.fold_in(key, 13)
    channel_scale = 0.25 * jnp.exp(jax.random.uniform(channel_key, (CO,), jnp.float32) * math.log(10.0))
    image_scale = jnp.exp(jnp.arange(BATCH, dtype=jnp.float32) / max(BATCH - 1, 1) * math.log(3.0))
    common = jnp.clip(jax.random.normal(common_key, (HH, WW, CO), jnp.float32), -3.0, 3.0)
    jitter = jnp.clip(jax.random.normal(jitter_key, (BATCH, HH, WW, CO), jnp.float32), -4.0, 4.0)
    jitter = jitter + 1.5 * common[None]
    return jitter * channel_scale * image_scale[:, None, None, None]


def shard_levels(own_key, dims, split, least, high):
    def one(axis_at, blocks):
        draws = jax.random.uniform(jax.random.fold_in(jax.random.fold_in(own_key, 6), axis_at), (blocks,), jnp.float32, least / len(split), high / len(split))
        return jnp.repeat(jnp.exp(draws), dims[axis_at] // blocks).reshape((-1,) + (1,) * (len(dims) - axis_at - 1))

    gain = one(*split[0])
    for cut in split[1:]:
        gain = gain * one(*cut)
    return gain


def normal_values(rng, extent, width, reach, pieces=(), kind=jnp.bfloat16):
    values = width * jax.random.normal(rng, extent, jnp.float32)
    if pieces:
        values = values * shard_levels(rng, extent, pieces, -0.22, 0.18)
    return jnp.clip(values, -reach, reach).astype(kind)


def setup_inputs(seed: int = 0) -> dict:
    streams_of = jax.random.split(jax.random.key(seed), 5)
    return {
        "inputs": draw_inputs(jax.random.fold_in(streams_of[4], 71), 0),
        "grad_out": draw_grad_out(jax.random.fold_in(streams_of[4], 71), 0),
        "weight": normal_values(streams_of[2], (CO, 3, 3, CI), (9 * CI) ** -0.5, 0.09375, ((0, 8),), jnp.float32),
        "momentum": normal_values(streams_of[3], (CO, 3, 3, CI), 1.0, 6.0, ((0, 512),), jnp.float32),
    }


EPSILON = 1e-06
MOMENTUM_RATE = 0.9
LEARN_RATE = 0.05

def pair_combine(left_term, right_term):
    cross_dot = lax.optimization_barrier(jnp.sum(left_term * right_term, axis=-1, keepdims=True))
    left_sq = lax.optimization_barrier(jnp.sum(left_term * left_term, axis=-1, keepdims=True))
    right_sq = lax.optimization_barrier(jnp.sum(right_term * right_term, axis=-1, keepdims=True))
    return (1.0 - cross_dot / (2.0 * (left_sq + EPSILON))) * left_term + (1.0 - cross_dot / (2.0 * (right_sq + EPSILON))) * right_term

def combine_tree(blocks):
    while blocks.shape[0] > 1:
        half_rows = blocks.shape[0] // 2
        blocks = pair_combine(blocks[:half_rows], blocks[half_rows:])
    return blocks[0]

def filter_grads(inputs, grad_out):
    images, height, across, chan_in = inputs.shape
    chan_out = grad_out.shape[3]
    padded = jnp.pad(inputs, ((0, 0), (1, 1), (1, 1), (0, 0)))
    grad_rows = grad_out.reshape(images * height * across, chan_out)
    tap_list = []
    for tap_row in range(3):
        for tap_col in range(3):
            window = padded[:, tap_row:tap_row + height, tap_col:tap_col + across, :].reshape(images * height * across, chan_in)
            tap_list.append(lax.dot_general(grad_rows, window, (((0,), (0,)), ((), ())), precision=lax.Precision.HIGHEST, preferred_element_type=jnp.float32))
    return jnp.stack(tap_list, axis=1).reshape(chan_out, 9 * chan_in)

def input_grads(grad_out, weight):
    images, height, across, chan_out = grad_out.shape
    padded = jnp.pad(grad_out, ((0, 0), (1, 1), (1, 1), (0, 0)))
    summed = jnp.zeros((images * height * across, weight.shape[3]), jnp.float32)
    for tap_row in range(3):
        for tap_col in range(3):
            window = padded[:, 2 - tap_row:2 - tap_row + height, 2 - tap_col:2 - tap_col + across, :].reshape(images * height * across, chan_out)
            summed = summed + jnp.dot(window, weight[:, tap_row, tap_col, :], precision=lax.Precision.HIGHEST, preferred_element_type=jnp.float32)
    return summed

def reference(inputs, grad_out, weight, momentum):
    images, height, across, chan_in = inputs.shape
    block_size = CO // N_CH
    rep_inputs = inputs.reshape(N_REP, IMG_DEV, height, across, chan_in)
    rep_grads = grad_out.reshape(N_REP, IMG_DEV, height, across, N_CH, block_size)

    def one_block(block_index):
        block_grad = lax.dynamic_index_in_dim(rep_grads, block_index, 4, keepdims=False)
        per_replica = jax.vmap(filter_grads)(rep_inputs, block_grad)
        return combine_tree(per_replica)
    combined = lax.map(one_block, jnp.arange(N_CH, dtype=jnp.int32)).reshape(CO, 3, 3, CI)
    norm_sq = jnp.sum(combined * combined)
    clip_scale = jnp.minimum(1.0, 0.5 * math.sqrt(CO * 9 * CI) / jnp.sqrt(norm_sq + EPSILON))
    new_momentum = MOMENTUM_RATE * momentum + clip_scale * combined
    new_weight = weight - LEARN_RATE * new_momentum
    input_grad = input_grads(grad_out, weight).reshape(images, height, across, chan_in)
    return (input_grad, new_weight, new_momentum)
```

```python
import math

import jax
import jax.numpy as jnp
from jax import lax
from jax.sharding import PartitionSpec as P

CO = 1024
CI = 512


EPSILON = 1e-06
MOMENTUM_RATE = 0.9
LEARN_RATE = 0.05
PREC = lax.Precision.HIGH


def filter_grads(inputs, grad_out):
    images, height, across, chan_in = inputs.shape
    chan_out = grad_out.shape[3]
    padded = jnp.pad(inputs, ((0, 0), (1, 1), (1, 1), (0, 0)))
    grad_rows = grad_out.reshape(images * height * across, chan_out)
    tap_list = []
    for tap_row in range(3):
        for tap_col in range(3):
            window = padded[:, tap_row : tap_row + height, tap_col : tap_col + across, :].reshape(
                images * height * across, chan_in
            )
            tap_list.append(
                lax.dot_general(
                    grad_rows,
                    window,
                    (((0,), (0,)), ((), ())),
                    precision=PREC,
                    preferred_element_type=jnp.float32,
                )
            )
    return jnp.stack(tap_list, axis=1)


def input_grads(grad_out, weight):
    images, height, across, chan_out = grad_out.shape
    padded = jnp.pad(grad_out, ((0, 0), (1, 1), (1, 1), (0, 0)))
    summed = jnp.zeros((images * height * across, weight.shape[3]), jnp.float32)
    for tap_row in range(3):
        for tap_col in range(3):
            window = padded[
                :, 2 - tap_row : 2 - tap_row + height, 2 - tap_col : 2 - tap_col + across, :
            ].reshape(images * height * across, chan_out)
            summed = summed + jnp.dot(
                window,
                weight[:, tap_row, tap_col, :],
                precision=PREC,
                preferred_element_type=jnp.float32,
            )
    return summed


def row_sums(value):
    rows = jnp.sum(value, axis=(1, 3))
    per = jnp.sum(rows.reshape(-1, 2, 4), axis=2, keepdims=True)
    return jnp.broadcast_to(per, per.shape[:2] + (4,)).reshape(-1, 1, 8, 1)


def pair_combine(left_term, right_term):
    cross_dot = row_sums(left_term * right_term)
    left_sq = row_sums(left_term * left_term)
    right_sq = row_sums(right_term * right_term)
    return (1.0 - cross_dot / (2.0 * (left_sq + EPSILON))) * left_term + (
        1.0 - cross_dot / (2.0 * (right_sq + EPSILON))
    ) * right_term


def global_sum(value, axes):
    for axis in axes:
        size = lax.axis_size(axis)
        spread = jnp.broadcast_to(value, (size, 1, 128))
        spread = lax.all_to_all(spread, axis, 0, 0, tiled=True)
        value = jnp.sum(spread[:, 0, 0])
    return value


def local(inputs, grad_out, weight, momentum):
    images, height, across, chan_in = inputs.shape
    chan_out = grad_out.shape[3]
    replicas = lax.axis_size("rep")
    planes = lax.axis_size("ch")
    col_count = chan_in // planes
    own_count = chan_out // replicas
    rep_index = lax.axis_index("rep")
    grads = filter_grads(inputs, grad_out)
    sent = (
        grads.reshape(replicas, own_count, 9, chan_in // 128, 128)
        .transpose(0, 2, 1, 3, 4)
        .reshape(replicas, 9, 8, 128)
    )
    current = lax.all_to_all(sent, "rep", 0, 0, tiled=True)

    flat_grad = input_grads(grad_out, weight)
    half = height * across
    parts = (
        flat_grad.reshape(images, half, planes, col_count)
        .transpose(2, 1, 0, 3)
        .reshape(planes, half, images * col_count)
    )
    parts = lax.all_to_all(parts, "ch", 0, 0, tiled=True)
    input_grad = (
        jnp.sum(parts, axis=0)
        .reshape(half, images, col_count)
        .transpose(1, 0, 2)
        .reshape(images, height, across, col_count)
    )

    while current.shape[0] > 1:
        upper = current.shape[0] // 2
        current = pair_combine(current[:upper], current[upper:])
    combined = (
        current.reshape(9, own_count, chan_in // 128, 128)
        .transpose(1, 0, 2, 3)
        .reshape(own_count, 3, 3, chan_in)
    )
    norm_sq = global_sum(jnp.sum(current * current), ("rep", "ch"))
    clip_scale = jnp.minimum(1.0, 0.5 * math.sqrt(CO * 9 * CI) / jnp.sqrt(norm_sq + EPSILON))
    owned_w = lax.dynamic_slice_in_dim(weight, rep_index * own_count, own_count, 0)
    new_momentum = MOMENTUM_RATE * momentum + clip_scale * combined
    new_weight = owned_w - LEARN_RATE * new_momentum
    return (input_grad, new_weight, new_momentum)


def solution(mesh):
    in_specs = (
        P("rep", None, None, None),
        P("rep", None, None, "ch"),
        P("ch", None, None, None),
        P(("ch", "rep"), None, None, None),
    )
    out_specs = (
        P("rep", None, None, "ch"),
        P(("ch", "rep"), None, None, None),
        P(("ch", "rep"), None, None, None),
    )
    return jax.shard_map(local, mesh=mesh, in_specs=in_specs, out_specs=out_specs, check_vma=False)
```

```python
import math

import jax
import jax.numpy as jnp
import numpy as np
from jax import lax
from jax.experimental import pallas as pl
from jax.experimental.pallas import tpu as pltpu
from jax.sharding import PartitionSpec as P

CO = 1024
CI = 512
EPSILON = 1e-06
MOMENTUM_RATE = 0.9
LEARN_RATE = 0.05
SIDE = 14
AREA = SIDE * SIDE
TAPS = [(row, col) for row in range(3) for col in range(3)]


def split_bf16(value):
    high = value.astype(jnp.bfloat16)
    low = (value - high.astype(jnp.float32)).astype(jnp.bfloat16)
    return high, low


def lane_masks():
    masks = np.zeros((16, 512), np.float32)
    for tap, (row, col) in enumerate(TAPS):
        for image in range(2):
            for pos in range(AREA):
                high, wide = pos // SIDE - (row - 1), pos % SIDE - (col - 1)
                if 0 <= high < SIDE and 0 <= wide < SIDE:
                    masks[tap, image * 256 + pos] = 1.0
    return masks


def row_masks():
    masks = np.zeros((2, 200, 128), np.float32)
    pos = np.arange(AREA) % SIDE
    masks[0, :AREA] = (pos + 1 < SIDE)[:, None]
    masks[1, :AREA] = (pos - 1 >= 0)[:, None]
    return masks


def grads_kernel(x_ref, d_ref, mask_ref, out_ref, x_hl, d_pad, d_t, lhs):
    d_pad[...] = jnp.zeros_like(d_pad)
    for image in range(2):
        d_pad[pl.ds(image * 256, AREA), :] = d_ref[pl.ds(image, AREA, stride=2), :]
    for part in range(4):
        d_t[part * 128 : (part + 1) * 128, :] = d_pad[part * 128 : (part + 1) * 128, :].T
    for image in range(2):
        for block in range(4):
            piece = x_ref[pl.ds(block * 2 + image, AREA, stride=8), :]
            piece = jnp.concatenate([piece, jnp.zeros((256 - AREA, 128), jnp.float32)], axis=0)
            high, low = split_bf16(piece)
            cols = slice(block * 128, (block + 1) * 128)
            x_hl[image * 256 : (image + 1) * 256, cols] = high
            x_hl[512 + image * 256 : 512 + (image + 1) * 256, cols] = low
    halves = []
    for odd in range(2):
        halves.append(
            jnp.concatenate(
                [d_t[pl.ds(part * 128 + odd, 64, stride=2), :] for part in range(4)], axis=1
            )
        )
    base = jnp.concatenate(halves, axis=0)
    for tap, (row, col) in enumerate(TAPS):
        shift = (row - 1) * SIDE + (col - 1)
        moved = jnp.concatenate(
            [
                pltpu.roll(base[:, image * 256 : (image + 1) * 256], shift % 256, 1)
                for image in range(2)
            ],
            axis=1,
        ) if shift else base
        if tap != 4:
            moved = moved * mask_ref[tap : tap + 1, :]
        high, low = split_bf16(moved)
        lhs[tap * 128 : (tap + 1) * 128, 0:512] = high
        lhs[tap * 128 : (tap + 1) * 128, 512:1024] = low
    x_high = x_hl[0:512, :]
    x_low = x_hl[512:1024, :]
    for start in range(0, 1152, 384):
        rows = slice(start, start + 384)
        acc = jnp.dot(lhs[rows, 0:512], x_high, preferred_element_type=jnp.float32)
        acc = acc + jnp.dot(lhs[rows, 512:1024], x_high, preferred_element_type=jnp.float32)
        acc = acc + jnp.dot(lhs[rows, 0:512], x_low, preferred_element_type=jnp.float32)
        for sub in range(3):
            tap = start // 128 + sub
            for odd in range(2):
                for block in range(4):
                    out_ref[pl.ds(tap * 8 + block * 2 + odd, 64, stride=72), :] = acc[
                        sub * 128 + odd * 64 : sub * 128 + odd * 64 + 64,
                        block * 128 : (block + 1) * 128,
                    ]


VM = pl.BlockSpec(memory_space=pltpu.VMEM)


def call_grads(x_rows, d_rows):
    return pl.pallas_call(
        grads_kernel,
        out_shape=jax.ShapeDtypeStruct((4608, 128), jnp.float32),
        in_specs=[VM, VM, VM],
        out_specs=VM,
        scratch_shapes=[
            pltpu.VMEM((1024, 512), jnp.bfloat16),
            pltpu.VMEM((512, 128), jnp.float32),
            pltpu.VMEM((512, 128), jnp.float32),
            pltpu.VMEM((1152, 1024), jnp.bfloat16),
        ],
        name="filter_grads",
        compiler_params=pltpu.CompilerParams(vmem_limit_bytes=20 * 1024 * 1024),
        cost_estimate=pl.CostEstimate(flops=3 * 2 * 1152 * 512 * 512, bytes_accessed=3500000, transcendentals=0),
    )(x_rows, d_rows, jnp.asarray(lane_masks()))


def input_kernel(d_ref, w_ref, mask_ref, out_ref, d_pad, lhs, w_hl):
    me = lax.axis_index("ch")
    d_pad[...] = jnp.zeros_like(d_pad)
    for image in range(2):
        d_pad[image, 16 : 16 + AREA, :] = d_ref[pl.ds(image, AREA, stride=2), :]
    for tap, (row, col) in enumerate(TAPS):
        shift = (row - 1) * SIDE + (col - 1)
        for image in range(2):
            moved = d_pad[image, 16 - shift : 216 - shift, :]
            if col == 0:
                moved = moved * mask_ref[0]
            if col == 2:
                moved = moved * mask_ref[1]
            high, low = split_bf16(moved)
            rows = slice(image * 208, image * 208 + 200)
            lhs[rows, tap * 128 : (tap + 1) * 128] = high
            lhs[rows, 1152 + tap * 128 : 1152 + (tap + 1) * 128] = low
    high, low = split_bf16(w_ref[...])
    w_hl[0] = high
    w_hl[1] = low
    lane = lax.broadcasted_iota(jnp.int32, (AREA, 128), 1)
    for pair in range(2):
        cols = slice(pair * 256, (pair + 1) * 256)
        acc = jnp.dot(lhs[:, 0:1152], w_hl[0, :, cols], preferred_element_type=jnp.float32)
        acc = acc + jnp.dot(lhs[:, 1152:2304], w_hl[0, :, cols], preferred_element_type=jnp.float32)
        acc = acc + jnp.dot(lhs[:, 0:1152], w_hl[1, :, cols], preferred_element_type=jnp.float32)
        for sub in range(2):
            first = acc[0:AREA, sub * 128 : (sub + 1) * 128]
            second = acc[208 : 208 + AREA, sub * 128 : (sub + 1) * 128]
            dest = pair * 4 + sub * 2
            out_ref[(dest + 8 - me) & 7] = jnp.where(lane < 64, first, pltpu.roll(second, 64, 1))
            out_ref[(dest + 9 - me) & 7] = jnp.where(lane < 64, pltpu.roll(first, 64, 1), second)


def call_input(d_rows, w_rows):
    return pl.pallas_call(
        input_kernel,
        out_shape=jax.ShapeDtypeStruct((8, AREA, 128), jnp.float32),
        in_specs=[VM, VM, VM],
        out_specs=VM,
        scratch_shapes=[
            pltpu.VMEM((2, 240, 128), jnp.float32),
            pltpu.VMEM((416, 2304), jnp.bfloat16),
            pltpu.VMEM((2, 1152, 512), jnp.bfloat16),
        ],
        name="input_grads",
        compiler_params=pltpu.CompilerParams(vmem_limit_bytes=20 * 1024 * 1024),
        cost_estimate=pl.CostEstimate(flops=3 * 2 * 416 * 1152 * 512, bytes_accessed=3500000, transcendentals=0),
    )(d_rows, w_rows, jnp.asarray(row_masks()))


def fold(value):
    value = value + pltpu.roll(value, 4, 1)
    value = value + pltpu.roll(value, 2, 1)
    return jnp.sum(value, axis=2, keepdims=True)


def tree_kernel(v_ref, out_ref, norm_ref, work):
    def pairs(src, dst, start, count, half):
        left = src[pl.ds(start, count)]
        right = src[pl.ds(start + half, count)]
        cross = fold(jnp.sum(left * right, axis=1))
        left_sq = fold(jnp.sum(left * left, axis=1))
        right_sq = fold(jnp.sum(right * right, axis=1))
        left_w = (1.0 - cross / (2.0 * (left_sq + EPSILON)))[:, None]
        right_w = (1.0 - cross / (2.0 * (right_sq + EPSILON)))[:, None]
        value = left_w * left + right_w * right
        dst[pl.ds(start, count)] = value
        return value

    half = 32
    src = v_ref
    while half > 1:
        count = min(half, 4)
        source = src

        def step(index, carry, source=source, count=count, half=half):
            pairs(source, work, index * count, count, half)
            return carry

        if half == count:
            step(0, 0)
        else:
            lax.fori_loop(0, half // count, step, 0)
        src = work
        half //= 2
    last = pairs(work, out_ref, 0, 1, 1)
    norm = jnp.sum(last[0] * last[0], axis=0)
    norm = jnp.sum(jnp.sum(norm, axis=1, keepdims=True), axis=0, keepdims=True)
    norm_ref[...] = jnp.broadcast_to(norm[None], norm_ref.shape)


def call_tree(vectors):
    return pl.pallas_call(
        tree_kernel,
        out_shape=(
            jax.ShapeDtypeStruct((1, 9, 8, 128), jnp.float32),
            jax.ShapeDtypeStruct((64, 1, 128), jnp.float32),
        ),
        in_specs=[VM],
        out_specs=(VM, VM),
        scratch_shapes=[pltpu.VMEM((32, 9, 8, 128), jnp.float32)],
        name="pair_tree",
        compiler_params=pltpu.CompilerParams(vmem_limit_bytes=10 * 1024 * 1024),
        cost_estimate=pl.CostEstimate(flops=64 * 9216 * 9, bytes_accessed=2400000, transcendentals=0),
    )(vectors)


def global_sum(spread):
    spread = lax.all_to_all(spread, "rep", 0, 0, tiled=True)
    value = jnp.sum(spread, axis=0, keepdims=True)
    planes = lax.axis_size("ch")
    spread = jnp.broadcast_to(value, (planes, 1, 128))
    spread = lax.all_to_all(spread, "ch", 0, 0, tiled=True)
    return jnp.sum(spread[:, 0, 0])


def local(inputs, grad_out, weight, momentum):
    images, height, across, chan_in = inputs.shape
    chan_out = grad_out.shape[3]
    replicas = lax.axis_size("rep")
    planes = lax.axis_size("ch")
    col_count = chan_in // planes
    own_count = chan_out // replicas
    rep_index = lax.axis_index("rep")
    x_rows = (
        inputs.transpose(1, 2, 0, 3)
        .reshape(AREA, images, 4, 128)
        .transpose(0, 2, 1, 3)
        .reshape(AREA * 8, 128)
    )
    d_rows = grad_out.transpose(1, 2, 0, 3).reshape(AREA * images, chan_out)
    w_rows = weight.transpose(1, 2, 0, 3).reshape(9 * chan_out, chan_in)
    sent = call_grads(x_rows, d_rows).reshape(replicas, 9, 8, 128)
    d_later, sent_held = lax.optimization_barrier((d_rows, sent))
    vectors = lax.all_to_all(sent_held, "rep", 0, 0, tiled=True)
    parts = call_input(d_later, w_rows)
    total = parts[0]
    for step in (4, 3, 5, 2, 6, 1, 7):
        pairs = [(source, (source + step) % planes) for source in range(planes)]
        total = total + lax.ppermute(parts[step], "ch", pairs)
    input_grad = (
        total
        .reshape(height, across, images, col_count)
        .transpose(2, 0, 1, 3)
    )

    owned_w = lax.dynamic_slice_in_dim(weight, rep_index * own_count, own_count, 0)
    vectors, input_grad, owned_w = lax.optimization_barrier((vectors, input_grad, owned_w))
    combined, spread = call_tree(vectors)
    combined = (
        combined.reshape(9, 4, own_count, 128)
        .transpose(2, 0, 1, 3)
        .reshape(own_count, 3, 3, chan_in)
    )
    norm_sq = global_sum(spread)
    clip_scale = jnp.minimum(1.0, 0.5 * math.sqrt(CO * 9 * CI) / jnp.sqrt(norm_sq + EPSILON))
    new_momentum = MOMENTUM_RATE * momentum + clip_scale * combined
    new_weight = owned_w - LEARN_RATE * new_momentum
    return (input_grad, new_weight, new_momentum)


def solution(mesh):
    in_specs = (
        P("rep", None, None, None),
        P("rep", None, None, "ch"),
        P("ch", None, None, None),
        P(("ch", "rep"), None, None, None),
    )
    out_specs = (
        P("rep", None, None, "ch"),
        P(("ch", "rep"), None, None, None),
        P(("ch", "rep"), None, None, None),
    )
    return jax.shard_map(local, mesh=mesh, in_specs=in_specs, out_specs=out_specs, check_vma=False)
```

```python
import math

import jax
import jax.numpy as jnp
import numpy as np
from jax import lax
from jax.experimental import pallas as pl
from jax.experimental.pallas import tpu as pltpu
from jax.sharding import PartitionSpec as P

CO = 1024
CI = 512
EPSILON = 1e-06
MOMENTUM_RATE = 0.9
LEARN_RATE = 0.05
SIDE = 14
AREA = SIDE * SIDE
TAPS = [(row, col) for row in range(3) for col in range(3)]


def split_bf16(value):
    high = value.astype(jnp.bfloat16)
    low = (value - high.astype(jnp.float32)).astype(jnp.bfloat16)
    return high, low


def lane_masks():
    masks = np.zeros((16, 512), np.float32)
    for tap, (row, col) in enumerate(TAPS):
        for image in range(2):
            for pos in range(AREA):
                high, wide = pos // SIDE - (row - 1), pos % SIDE - (col - 1)
                if 0 <= high < SIDE and 0 <= wide < SIDE:
                    masks[tap, image * 256 + pos] = 1.0
    return masks


def row_masks():
    masks = np.zeros((2, 200, 128), np.float32)
    pos = np.arange(AREA) % SIDE
    masks[0, :AREA] = (pos + 1 < SIDE)[:, None]
    masks[1, :AREA] = (pos - 1 >= 0)[:, None]
    return masks


def grads_kernel(x_hbm, d_hbm, mask_hbm, out_hbm, x_in, d_in, mask_ref, x_hl, d_pad, d_t, lhs, out_a, out_b, out_c, in_sem, out_sem):
    d_copy = pltpu.make_async_copy(d_hbm, d_in, in_sem.at[0])
    x_copy = pltpu.make_async_copy(x_hbm, x_in, in_sem.at[1])
    mask_copy = pltpu.make_async_copy(mask_hbm, mask_ref, in_sem.at[2])
    d_copy.start()
    mask_copy.start()
    x_copy.start()
    d_pad[...] = jnp.zeros_like(d_pad)
    d_copy.wait()
    for image in range(2):
        d_pad[pl.ds(image * 256, AREA), :] = d_in[pl.ds(image, AREA, stride=2), :]
    for part in range(4):
        d_t[part * 128 : (part + 1) * 128, :] = d_pad[part * 128 : (part + 1) * 128, :].T
    halves = []
    for odd in range(2):
        halves.append(
            jnp.concatenate(
                [d_t[pl.ds(part * 128 + odd, 64, stride=2), :] for part in range(4)], axis=1
            )
        )
    base = jnp.concatenate(halves, axis=0)
    mask_copy.wait()
    for tap, (row, col) in enumerate(TAPS):
        shift = (row - 1) * SIDE + (col - 1)
        moved = jnp.concatenate(
            [
                pltpu.roll(base[:, image * 256 : (image + 1) * 256], shift % 256, 1)
                for image in range(2)
            ],
            axis=1,
        ) if shift else base
        if tap != 4:
            moved = moved * mask_ref[tap : tap + 1, :]
        high, low = split_bf16(moved)
        lhs[tap * 128 : (tap + 1) * 128, 0:512] = high
        lhs[tap * 128 : (tap + 1) * 128, 512:1024] = low
    x_copy.wait()
    for image in range(2):
        for block in range(4):
            piece = x_in[pl.ds(block * 2 + image, AREA, stride=8), :]
            piece = jnp.concatenate([piece, jnp.zeros((256 - AREA, 128), jnp.float32)], axis=0)
            high, low = split_bf16(piece)
            cols = slice(block * 128, (block + 1) * 128)
            x_hl[image * 256 : (image + 1) * 256, cols] = high
            x_hl[512 + image * 256 : 512 + (image + 1) * 256, cols] = low
    x_high = x_hl[0:512, :]
    x_low = x_hl[512:1024, :]
    copies = []
    for group, out in enumerate((out_a, out_b, out_c)):
        rows = slice(group * 384, group * 384 + 384)
        acc = jnp.dot(lhs[rows, 0:512], x_high, preferred_element_type=jnp.float32)
        acc = acc + jnp.dot(lhs[rows, 512:1024], x_high, preferred_element_type=jnp.float32)
        acc = acc + jnp.dot(lhs[rows, 0:512], x_low, preferred_element_type=jnp.float32)
        for sub in range(3):
            for odd in range(2):
                for block in range(4):
                    out[pl.ds(sub * 8 + block * 2 + odd, 64, stride=24), :] = acc[
                        sub * 128 + odd * 64 : sub * 128 + odd * 64 + 64,
                        block * 128 : (block + 1) * 128,
                    ]
        copy = pltpu.make_async_copy(
            out.reshape(64, 24, 128), out_hbm.at[:, pl.ds(group * 24, 24), :], out_sem.at[group]
        )
        copy.start()
        copies.append(copy)
    for copy in copies:
        copy.wait()


VM = pl.BlockSpec(memory_space=pltpu.VMEM)


ANY = pl.BlockSpec(memory_space=pl.ANY)


def call_grads(x_rows, d_rows):
    return pl.pallas_call(
        grads_kernel,
        out_shape=jax.ShapeDtypeStruct((64, 72, 128), jnp.float32),
        in_specs=[ANY, ANY, ANY],
        out_specs=ANY,
        scratch_shapes=[
            pltpu.VMEM((AREA * 8, 128), jnp.float32),
            pltpu.VMEM((AREA * 2, 128), jnp.float32),
            pltpu.VMEM((16, 512), jnp.float32),
            pltpu.VMEM((1024, 512), jnp.bfloat16),
            pltpu.VMEM((512, 128), jnp.float32),
            pltpu.VMEM((512, 128), jnp.float32),
            pltpu.VMEM((1152, 1024), jnp.bfloat16),
            pltpu.VMEM((1536, 128), jnp.float32),
            pltpu.VMEM((1536, 128), jnp.float32),
            pltpu.VMEM((1536, 128), jnp.float32),
            pltpu.SemaphoreType.DMA((3,)),
            pltpu.SemaphoreType.DMA((3,)),
        ],
        name="filter_grads",
        cost_estimate=pl.CostEstimate(
            flops=3 * 2 * 1152 * 512 * 512, bytes_accessed=3500000, transcendentals=0
        ),
    )(x_rows, d_rows, jnp.asarray(lane_masks()))


def input_kernel(d_ref, w_ref, mask_ref, out_ref, d_pad, lhs, w_hl):
    me = lax.axis_index("ch")
    d_pad[...] = jnp.zeros_like(d_pad)
    for image in range(2):
        d_pad[image, 16 : 16 + AREA, :] = d_ref[pl.ds(image, AREA, stride=2), :]
    for tap, (row, col) in enumerate(TAPS):
        shift = (row - 1) * SIDE + (col - 1)
        for image in range(2):
            moved = d_pad[image, 16 - shift : 216 - shift, :]
            if col == 0:
                moved = moved * mask_ref[0]
            if col == 2:
                moved = moved * mask_ref[1]
            high, low = split_bf16(moved)
            rows = slice(image * 208, image * 208 + 200)
            lhs[rows, tap * 128 : (tap + 1) * 128] = high
            lhs[rows, 1152 + tap * 128 : 1152 + (tap + 1) * 128] = low
    high, low = split_bf16(w_ref[...])
    w_hl[0] = high
    w_hl[1] = low
    lane = lax.broadcasted_iota(jnp.int32, (AREA, 128), 1)
    for pair in range(2):
        cols = slice(pair * 256, (pair + 1) * 256)
        acc = jnp.dot(lhs[:, 0:1152], w_hl[0, :, cols], preferred_element_type=jnp.float32)
        acc = acc + jnp.dot(lhs[:, 1152:2304], w_hl[0, :, cols], preferred_element_type=jnp.float32)
        acc = acc + jnp.dot(lhs[:, 0:1152], w_hl[1, :, cols], preferred_element_type=jnp.float32)
        for sub in range(2):
            first = acc[0:AREA, sub * 128 : (sub + 1) * 128]
            second = acc[208 : 208 + AREA, sub * 128 : (sub + 1) * 128]
            dest = pair * 4 + sub * 2
            out_ref[(dest + 8 - me) & 7] = jnp.where(lane < 64, first, pltpu.roll(second, 64, 1))
            out_ref[(dest + 9 - me) & 7] = jnp.where(lane < 64, pltpu.roll(first, 64, 1), second)


def call_input(d_rows, w_rows):
    return pl.pallas_call(
        input_kernel,
        out_shape=jax.ShapeDtypeStruct((8, AREA, 128), jnp.float32),
        in_specs=[VM, VM, VM],
        out_specs=VM,
        scratch_shapes=[
            pltpu.VMEM((2, 240, 128), jnp.float32),
            pltpu.VMEM((416, 2304), jnp.bfloat16),
            pltpu.VMEM((2, 1152, 512), jnp.bfloat16),
        ],
        name="input_grads",
        compiler_params=pltpu.CompilerParams(vmem_limit_bytes=20 * 1024 * 1024),
        cost_estimate=pl.CostEstimate(flops=3 * 2 * 416 * 1152 * 512, bytes_accessed=3500000, transcendentals=0),
    )(d_rows, w_rows, jnp.asarray(row_masks()))


def fold(value):
    value = value + pltpu.roll(value, 4, 1)
    value = value + pltpu.roll(value, 2, 1)
    return jnp.sum(value, axis=2, keepdims=True)


def tree_kernel(v_ref, out_ref, norm_ref, work):
    def pairs(src, dst, start, count, half):
        left = src[pl.ds(start, count)]
        right = src[pl.ds(start + half, count)]
        cross = fold(jnp.sum(left * right, axis=1))
        left_sq = fold(jnp.sum(left * left, axis=1))
        right_sq = fold(jnp.sum(right * right, axis=1))
        left_w = (1.0 - cross / (2.0 * (left_sq + EPSILON)))[:, None]
        right_w = (1.0 - cross / (2.0 * (right_sq + EPSILON)))[:, None]
        value = left_w * left + right_w * right
        dst[pl.ds(start, count)] = value
        return value

    half = 32
    src = v_ref
    while half > 1:
        count = min(half, 4)
        source = src

        def step(index, carry, source=source, count=count, half=half):
            pairs(source, work, index * count, count, half)
            return carry

        if half == count:
            step(0, 0)
        else:
            lax.fori_loop(0, half // count, step, 0)
        src = work
        half //= 2
    last = pairs(work, out_ref, 0, 1, 1)
    norm = jnp.sum(last[0] * last[0], axis=0)
    norm = jnp.sum(jnp.sum(norm, axis=1, keepdims=True), axis=0, keepdims=True)
    norm_ref[...] = jnp.broadcast_to(norm[None], norm_ref.shape)


def call_tree(vectors):
    return pl.pallas_call(
        tree_kernel,
        out_shape=(
            jax.ShapeDtypeStruct((1, 9, 8, 128), jnp.float32),
            jax.ShapeDtypeStruct((64, 1, 128), jnp.float32),
        ),
        in_specs=[VM],
        out_specs=(VM, VM),
        scratch_shapes=[pltpu.VMEM((32, 9, 8, 128), jnp.float32)],
        name="pair_tree",
        compiler_params=pltpu.CompilerParams(vmem_limit_bytes=10 * 1024 * 1024),
        cost_estimate=pl.CostEstimate(flops=64 * 9216 * 9, bytes_accessed=2400000, transcendentals=0),
    )(vectors)


def update_kernel(terms_ref, combined_ref, weight_ref, momentum_ref, weight_out, momentum_out):
    norm_sq = jnp.sum(terms_ref[...], axis=0)
    clip_scale = jnp.minimum(
        1.0, 0.5 * math.sqrt(CO * 9 * CI) / jnp.sqrt(norm_sq + EPSILON)
    )
    scale = jnp.broadcast_to(clip_scale, (8, 128))[None]
    new_momentum = MOMENTUM_RATE * momentum_ref[...] + scale * combined_ref[...]
    momentum_out[...] = new_momentum
    weight_out[...] = weight_ref[...] - LEARN_RATE * new_momentum


def call_update(terms, combined, weight, momentum):
    return pl.pallas_call(
        update_kernel,
        out_shape=(jax.ShapeDtypeStruct((9, 8, 128), jnp.float32),) * 2,
        in_specs=[VM] * 4,
        out_specs=(VM, VM),
        name="update",
        compiler_params=pltpu.CompilerParams(vmem_limit_bytes=2 * 1024 * 1024),
    )(terms, combined, weight, momentum)


def norm_terms(spread):
    spread = lax.all_to_all(spread, "rep", 0, 0, tiled=True)
    value = jnp.sum(spread, axis=0, keepdims=True)
    planes = lax.axis_size("ch")
    spread = jnp.broadcast_to(value, (planes, 1, 128))
    return lax.all_to_all(spread, "ch", 0, 0, tiled=True)


def own_rows(value):
    return value.transpose(1, 2, 0, 3).reshape(9, 2, 4, 128).transpose(0, 2, 1, 3).reshape(9, 8, 128)


def whole_rows(value):
    return value.reshape(9, 4, 2, 128).transpose(0, 2, 1, 3).reshape(3, 3, 2, 512).transpose(2, 0, 1, 3)


def local(inputs, grad_out, weight, momentum):
    images, height, across, chan_in = inputs.shape
    chan_out = grad_out.shape[3]
    replicas = lax.axis_size("rep")
    planes = lax.axis_size("ch")
    col_count = chan_in // planes
    own_count = chan_out // replicas
    rep_index = lax.axis_index("rep")
    x_rows = (
        inputs.transpose(1, 2, 0, 3)
        .reshape(AREA, images, 4, 128)
        .transpose(0, 2, 1, 3)
        .reshape(AREA * 8, 128)
    )
    d_rows = grad_out.transpose(1, 2, 0, 3).reshape(AREA * images, chan_out)
    w_rows = weight.transpose(1, 2, 0, 3).reshape(9 * chan_out, chan_in)
    sent = call_grads(x_rows, d_rows).reshape(replicas, 9, 8, 128)
    d_later, sent_held = lax.optimization_barrier((d_rows, sent))
    vectors = lax.all_to_all(sent_held, "rep", 0, 0, tiled=True)
    parts = call_input(d_later, w_rows)
    total = parts[0]
    for step in (4, 3, 5, 2, 6, 1, 7):
        pairs = [(source, (source + step) % planes) for source in range(planes)]
        total = total + lax.ppermute(parts[step], "ch", pairs)
    input_grad = (
        total
        .reshape(height, across, images, col_count)
        .transpose(2, 0, 1, 3)
    )

    owned_w = lax.dynamic_slice_in_dim(weight, rep_index * own_count, own_count, 0)
    vectors, input_grad, owned_w = lax.optimization_barrier((vectors, input_grad, owned_w))
    combined, spread = call_tree(vectors)
    terms = norm_terms(spread)
    new_weight, new_momentum = call_update(
        terms, combined[0], own_rows(owned_w), own_rows(momentum)
    )
    new_weight, new_momentum = whole_rows(new_weight), whole_rows(new_momentum)
    return (input_grad, new_weight, new_momentum)


def solution(mesh):
    in_specs = (
        P("rep", None, None, None),
        P("rep", None, None, "ch"),
        P("ch", None, None, None),
        P(("ch", "rep"), None, None, None),
    )
    out_specs = (
        P("rep", None, None, "ch"),
        P(("ch", "rep"), None, None, None),
        P(("ch", "rep"), None, None, None),
    )
    return jax.shard_map(local, mesh=mesh, in_specs=in_specs, out_specs=out_specs, check_vma=False)
```

```python
import math

import jax
import jax.numpy as jnp
import numpy as np
from jax import lax
from jax.experimental import pallas as pl
from jax.experimental.pallas import tpu as pltpu
from jax.sharding import PartitionSpec as P

CO = 1024
CI = 512
EPSILON = 1e-06
MOMENTUM_RATE = 0.9
LEARN_RATE = 0.05
SIDE = 14
AREA = SIDE * SIDE
TAPS = [(row, col) for row in range(3) for col in range(3)]


def split_bf16(value):
    high = value.astype(jnp.bfloat16)
    low = (value - high.astype(jnp.float32)).astype(jnp.bfloat16)
    return high, low


def lane_masks():
    masks = np.zeros((16, 512), np.float32)
    for tap, (row, col) in enumerate(TAPS):
        for image in range(2):
            for pos in range(AREA):
                high, wide = pos // SIDE - (row - 1), pos % SIDE - (col - 1)
                if 0 <= high < SIDE and 0 <= wide < SIDE:
                    masks[tap, image * 256 + pos] = 1.0
    return masks


def row_masks():
    masks = np.zeros((2, 200, 128), np.float32)
    pos = np.arange(AREA) % SIDE
    masks[0, :AREA] = (pos + 1 < SIDE)[:, None]
    masks[1, :AREA] = (pos - 1 >= 0)[:, None]
    return masks


def grads_kernel(x_hbm, d_hbm, mask_hbm, out_hbm, x_in, d_in, mask_ref, x_hl, d_pad, d_t, lhs, out_a, out_b, out_c, in_sem, out_sem):
    d_copy = pltpu.make_async_copy(d_hbm, d_in, in_sem.at[0])
    x_copy = pltpu.make_async_copy(x_hbm, x_in, in_sem.at[1])
    mask_copy = pltpu.make_async_copy(mask_hbm, mask_ref, in_sem.at[2])
    d_copy.start()
    mask_copy.start()
    x_copy.start()
    d_pad[...] = jnp.zeros_like(d_pad)
    d_copy.wait()
    for image in range(2):
        d_pad[pl.ds(image * 256, AREA), :] = d_in[pl.ds(image, AREA, stride=2), :]
    for part in range(4):
        d_t[part * 128 : (part + 1) * 128, :] = d_pad[part * 128 : (part + 1) * 128, :].T
    halves = []
    for odd in range(2):
        halves.append(
            jnp.concatenate(
                [d_t[pl.ds(part * 128 + odd, 64, stride=2), :] for part in range(4)], axis=1
            )
        )
    base = jnp.concatenate(halves, axis=0)
    mask_copy.wait()

    def fill(taps):
        for tap in taps:
            row, col = TAPS[tap]
            shift = (row - 1) * SIDE + (col - 1)
            moved = base
            if shift:
                moved = jnp.concatenate(
                    [
                        pltpu.roll(base[:, image * 256 : (image + 1) * 256], shift % 256, 1)
                        for image in range(2)
                    ],
                    axis=1,
                )
                moved = moved * mask_ref[tap : tap + 1, :]
            high, low = split_bf16(moved)
            lhs[tap * 128 : (tap + 1) * 128, 0:512] = high
            lhs[tap * 128 : (tap + 1) * 128, 512:1024] = low

    fill(range(0, 3))
    x_copy.wait()
    for image in range(2):
        for block in range(4):
            piece = x_in[pl.ds(block * 2 + image, AREA, stride=8), :]
            piece = jnp.concatenate([piece, jnp.zeros((256 - AREA, 128), jnp.float32)], axis=0)
            high, low = split_bf16(piece)
            cols = slice(block * 128, (block + 1) * 128)
            x_hl[image * 256 : (image + 1) * 256, cols] = high
            x_hl[512 + image * 256 : 512 + (image + 1) * 256, cols] = low
    x_high = x_hl[0:512, :]
    x_low = x_hl[512:1024, :]
    copies = []
    for group, out in enumerate((out_a, out_b, out_c)):
        if group < 2:
            fill(range(group * 3 + 3, group * 3 + 6))
        rows = slice(group * 384, group * 384 + 384)
        acc = jnp.dot(lhs[rows, 0:512], x_high, preferred_element_type=jnp.float32)
        acc = acc + jnp.dot(lhs[rows, 512:1024], x_high, preferred_element_type=jnp.float32)
        acc = acc + jnp.dot(lhs[rows, 0:512], x_low, preferred_element_type=jnp.float32)
        for sub in range(3):
            for odd in range(2):
                for block in range(4):
                    out[pl.ds(sub * 8 + block * 2 + odd, 64, stride=24), :] = acc[
                        sub * 128 + odd * 64 : sub * 128 + odd * 64 + 64,
                        block * 128 : (block + 1) * 128,
                    ]
        copy = pltpu.make_async_copy(
            out.reshape(64, 24, 128), out_hbm.at[:, pl.ds(group * 24, 24), :], out_sem.at[group]
        )
        copy.start()
        copies.append(copy)
    for copy in copies:
        copy.wait()


VM = pl.BlockSpec(memory_space=pltpu.VMEM)


ANY = pl.BlockSpec(memory_space=pl.ANY)


def call_grads(x_rows, d_rows):
    return pl.pallas_call(
        grads_kernel,
        out_shape=jax.ShapeDtypeStruct((64, 72, 128), jnp.float32),
        in_specs=[ANY, ANY, ANY],
        out_specs=ANY,
        scratch_shapes=[
            pltpu.VMEM((AREA * 8, 128), jnp.float32),
            pltpu.VMEM((AREA * 2, 128), jnp.float32),
            pltpu.VMEM((16, 512), jnp.float32),
            pltpu.VMEM((1024, 512), jnp.bfloat16),
            pltpu.VMEM((512, 128), jnp.float32),
            pltpu.VMEM((512, 128), jnp.float32),
            pltpu.VMEM((1152, 1024), jnp.bfloat16),
            pltpu.VMEM((1536, 128), jnp.float32),
            pltpu.VMEM((1536, 128), jnp.float32),
            pltpu.VMEM((1536, 128), jnp.float32),
            pltpu.SemaphoreType.DMA((3,)),
            pltpu.SemaphoreType.DMA((3,)),
        ],
        name="filter_grads",
        cost_estimate=pl.CostEstimate(
            flops=3 * 2 * 1152 * 512 * 512, bytes_accessed=3500000, transcendentals=0
        ),
    )(x_rows, d_rows, jnp.asarray(lane_masks()))


def input_kernel(d_ref, w_ref, mask_ref, out_ref, d_pad, lhs, w_hl):
    me = lax.axis_index("ch")
    d_pad[...] = jnp.zeros_like(d_pad)
    for image in range(2):
        d_pad[image, 16 : 16 + AREA, :] = d_ref[pl.ds(image, AREA, stride=2), :]
    for tap, (row, col) in enumerate(TAPS):
        shift = (row - 1) * SIDE + (col - 1)
        for image in range(2):
            moved = d_pad[image, 16 - shift : 216 - shift, :]
            if col == 0:
                moved = moved * mask_ref[0]
            if col == 2:
                moved = moved * mask_ref[1]
            high, low = split_bf16(moved)
            rows = slice(image * 208, image * 208 + 200)
            lhs[rows, tap * 128 : (tap + 1) * 128] = high
            lhs[rows, 1152 + tap * 128 : 1152 + (tap + 1) * 128] = low
    high, low = split_bf16(w_ref[...])
    w_hl[0] = high
    w_hl[1] = low
    lane = lax.broadcasted_iota(jnp.int32, (AREA, 128), 1)
    for pair in range(2):
        cols = slice(pair * 256, (pair + 1) * 256)
        acc = jnp.dot(lhs[:, 0:1152], w_hl[0, :, cols], preferred_element_type=jnp.float32)
        acc = acc + jnp.dot(lhs[:, 1152:2304], w_hl[0, :, cols], preferred_element_type=jnp.float32)
        acc = acc + jnp.dot(lhs[:, 0:1152], w_hl[1, :, cols], preferred_element_type=jnp.float32)
        for sub in range(2):
            first = acc[0:AREA, sub * 128 : (sub + 1) * 128]
            second = acc[208 : 208 + AREA, sub * 128 : (sub + 1) * 128]
            dest = pair * 4 + sub * 2
            out_ref[(dest + 8 - me) & 7] = jnp.where(lane < 64, first, pltpu.roll(second, 64, 1))
            out_ref[(dest + 9 - me) & 7] = jnp.where(lane < 64, pltpu.roll(first, 64, 1), second)


def call_input(d_rows, w_rows):
    return pl.pallas_call(
        input_kernel,
        out_shape=jax.ShapeDtypeStruct((8, AREA, 128), jnp.float32),
        in_specs=[VM, VM, VM],
        out_specs=VM,
        scratch_shapes=[
            pltpu.VMEM((2, 240, 128), jnp.float32),
            pltpu.VMEM((416, 2304), jnp.bfloat16),
            pltpu.VMEM((2, 1152, 512), jnp.bfloat16),
        ],
        name="input_grads",
        compiler_params=pltpu.CompilerParams(vmem_limit_bytes=20 * 1024 * 1024),
        cost_estimate=pl.CostEstimate(flops=3 * 2 * 416 * 1152 * 512, bytes_accessed=3500000, transcendentals=0),
    )(d_rows, w_rows, jnp.asarray(row_masks()))


def fold(value):
    value = value + pltpu.roll(value, 4, 1)
    value = value + pltpu.roll(value, 2, 1)
    return jnp.sum(value, axis=2, keepdims=True)


def pair_weights(cross, left_sq, right_sq):
    count = len(cross)
    sums = fold(jnp.stack(cross + left_sq + right_sq, axis=0))
    cross, left_sq, right_sq = sums[:count], sums[count : 2 * count], sums[2 * count :]
    left_w = 1.0 - cross / (2.0 * (left_sq + EPSILON))
    right_w = 1.0 - cross / (2.0 * (right_sq + EPSILON))
    return left_w, right_w


def tree_kernel(v_ref, out_ref, norm_ref, work):
    half = 32
    cross, left_sq, right_sq = [], [], []
    for index in range(half):
        left, right = v_ref[index], v_ref[index + half]
        cross.append(jnp.sum(left * right, axis=0))
        left_sq.append(jnp.sum(left * left, axis=0))
        right_sq.append(jnp.sum(right * right, axis=0))
    src = v_ref
    while half > 1:
        left_w, right_w = pair_weights(cross, left_sq, right_sq)
        cross, left_sq, right_sq = [], [], []
        quarter = half // 2
        for index in range(quarter):
            made = []
            for place in (index, index + quarter):
                value = left_w[place] * src[place] + right_w[place] * src[place + half]
                work[place] = value
                made.append(value)
            left, right = made
            cross.append(jnp.sum(left * right, axis=0))
            left_sq.append(jnp.sum(left * left, axis=0))
            right_sq.append(jnp.sum(right * right, axis=0))
        src = work
        half = quarter
    left_w, right_w = pair_weights(cross, left_sq, right_sq)
    last = left_w[0] * work[0] + right_w[0] * work[1]
    out_ref[0] = last
    norm = jnp.sum(last * last, axis=0)
    norm = jnp.sum(jnp.sum(norm, axis=1, keepdims=True), axis=0, keepdims=True)
    norm_ref[...] = jnp.broadcast_to(norm[None], norm_ref.shape)


def call_tree(vectors):
    return pl.pallas_call(
        tree_kernel,
        out_shape=(
            jax.ShapeDtypeStruct((1, 9, 8, 128), jnp.float32),
            jax.ShapeDtypeStruct((64, 1, 128), jnp.float32),
        ),
        in_specs=[VM],
        out_specs=(VM, VM),
        scratch_shapes=[pltpu.VMEM((32, 9, 8, 128), jnp.float32)],
        name="pair_tree",
        compiler_params=pltpu.CompilerParams(vmem_limit_bytes=10 * 1024 * 1024),
        cost_estimate=pl.CostEstimate(flops=64 * 9216 * 9, bytes_accessed=2400000, transcendentals=0),
    )(vectors)


def update_kernel(terms_ref, combined_ref, weight_ref, momentum_ref, weight_out, momentum_out):
    norm_sq = jnp.sum(terms_ref[...], axis=0)
    clip_scale = jnp.minimum(
        1.0, 0.5 * math.sqrt(CO * 9 * CI) / jnp.sqrt(norm_sq + EPSILON)
    )
    scale = jnp.broadcast_to(clip_scale, (8, 128))[None]
    new_momentum = MOMENTUM_RATE * momentum_ref[...] + scale * combined_ref[...]
    momentum_out[...] = new_momentum
    weight_out[...] = weight_ref[...] - LEARN_RATE * new_momentum


def call_update(terms, combined, weight, momentum):
    return pl.pallas_call(
        update_kernel,
        out_shape=(jax.ShapeDtypeStruct((9, 8, 128), jnp.float32),) * 2,
        in_specs=[VM] * 4,
        out_specs=(VM, VM),
        name="update",
        compiler_params=pltpu.CompilerParams(vmem_limit_bytes=2 * 1024 * 1024),
    )(terms, combined, weight, momentum)


def norm_terms(spread):
    spread = lax.all_to_all(spread, "rep", 0, 0, tiled=True)
    value = jnp.sum(spread, axis=0, keepdims=True)
    planes = lax.axis_size("ch")
    spread = jnp.broadcast_to(value, (planes, 1, 128))
    return lax.all_to_all(spread, "ch", 0, 0, tiled=True)


def own_rows(value):
    return value.transpose(1, 2, 0, 3).reshape(9, 2, 4, 128).transpose(0, 2, 1, 3).reshape(9, 8, 128)


def whole_rows(value):
    return value.reshape(9, 4, 2, 128).transpose(0, 2, 1, 3).reshape(3, 3, 2, 512).transpose(2, 0, 1, 3)


def local(inputs, grad_out, weight, momentum):
    images, height, across, chan_in = inputs.shape
    chan_out = grad_out.shape[3]
    replicas = lax.axis_size("rep")
    planes = lax.axis_size("ch")
    col_count = chan_in // planes
    own_count = chan_out // replicas
    rep_index = lax.axis_index("rep")
    x_rows = (
        inputs.transpose(1, 2, 0, 3)
        .reshape(AREA, images, 4, 128)
        .transpose(0, 2, 1, 3)
        .reshape(AREA * 8, 128)
    )
    d_rows = grad_out.transpose(1, 2, 0, 3).reshape(AREA * images, chan_out)
    w_rows = weight.transpose(1, 2, 0, 3).reshape(9 * chan_out, chan_in)
    sent = call_grads(x_rows, d_rows).reshape(replicas, 9, 8, 128)
    d_later, sent_held = lax.optimization_barrier((d_rows, sent))
    vectors = lax.all_to_all(sent_held, "rep", 0, 0, tiled=True)
    parts = call_input(d_later, w_rows)
    total = parts[0]
    for step in (4, 3, 5, 2, 6, 1, 7):
        pairs = [(source, (source + step) % planes) for source in range(planes)]
        total = total + lax.ppermute(parts[step], "ch", pairs)
    input_grad = (
        total
        .reshape(height, across, images, col_count)
        .transpose(2, 0, 1, 3)
    )

    owned_w = lax.dynamic_slice_in_dim(weight, rep_index * own_count, own_count, 0)
    vectors, input_grad, owned_w = lax.optimization_barrier((vectors, input_grad, owned_w))
    combined, spread = call_tree(vectors)
    terms = norm_terms(spread)
    new_weight, new_momentum = call_update(
        terms, combined[0], own_rows(owned_w), own_rows(momentum)
    )
    new_weight, new_momentum = whole_rows(new_weight), whole_rows(new_momentum)
    return (input_grad, new_weight, new_momentum)


def solution(mesh):
    in_specs = (
        P("rep", None, None, None),
        P("rep", None, None, "ch"),
        P("ch", None, None, None),
        P(("ch", "rep"), None, None, None),
    )
    out_specs = (
        P("rep", None, None, "ch"),
        P(("ch", "rep"), None, None, None),
        P(("ch", "rep"), None, None, None),
    )
    return jax.shard_map(local, mesh=mesh, in_specs=in_specs, out_specs=out_specs, check_vma=False)
```

```python
import math

import jax
import jax.numpy as jnp
import numpy as np
from jax import lax
from jax.experimental import pallas as pl
from jax.experimental.pallas import tpu as pltpu
from jax.sharding import PartitionSpec as P

CO = 1024
CI = 512
EPSILON = 1e-06
MOMENTUM_RATE = 0.9
LEARN_RATE = 0.05
SIDE = 14
REP = ("y", "x", "core")
AREA = SIDE * SIDE
TAPS = [(row, col) for row in range(3) for col in range(3)]


def split_bf16(value):
    high = value.astype(jnp.bfloat16)
    low = (value - high.astype(jnp.float32)).astype(jnp.bfloat16)
    return high, low


def lane_masks():
    masks = np.zeros((16, 512), np.float32)
    for tap, (row, col) in enumerate(TAPS):
        for image in range(2):
            for pos in range(AREA):
                high, wide = pos // SIDE - (row - 1), pos % SIDE - (col - 1)
                if 0 <= high < SIDE and 0 <= wide < SIDE:
                    masks[tap, image * 256 + pos] = 1.0
    return masks


def row_masks():
    masks = np.zeros((2, 200, 128), np.float32)
    pos = np.arange(AREA) % SIDE
    masks[0, :AREA] = (pos + 1 < SIDE)[:, None]
    masks[1, :AREA] = (pos - 1 >= 0)[:, None]
    return masks


def grads_kernel(x_hbm, d_hbm, mask_hbm, out_hbm, x_in, d_in, mask_ref, x_hl, d_pad, d_t, lhs, out_a, out_b, out_c, in_sem, out_sem):
    d_copy = pltpu.make_async_copy(d_hbm, d_in, in_sem.at[0])
    x_copy = pltpu.make_async_copy(x_hbm, x_in, in_sem.at[1])
    mask_copy = pltpu.make_async_copy(mask_hbm, mask_ref, in_sem.at[2])
    d_copy.start()
    mask_copy.start()
    x_copy.start()
    d_pad[...] = jnp.zeros_like(d_pad)
    d_copy.wait()
    for image in range(2):
        d_pad[pl.ds(image * 256, AREA), :] = d_in[pl.ds(image, AREA, stride=2), :]
    for part in range(4):
        d_t[part * 128 : (part + 1) * 128, :] = d_pad[part * 128 : (part + 1) * 128, :].T
    halves = []
    for odd in range(2):
        for spot in range(8):
            halves.append(
                jnp.concatenate(
                    [
                        d_t[pl.ds(part * 128 + spot * 2 + odd, 8, stride=16), :]
                        for part in range(4)
                    ],
                    axis=1,
                )
            )
    base = jnp.concatenate(halves, axis=0)
    mask_copy.wait()

    def fill(taps):
        for tap in taps:
            row, col = TAPS[tap]
            shift = (row - 1) * SIDE + (col - 1)
            moved = base
            if shift:
                moved = jnp.concatenate(
                    [
                        pltpu.roll(base[:, image * 256 : (image + 1) * 256], shift % 256, 1)
                        for image in range(2)
                    ],
                    axis=1,
                )
                moved = moved * mask_ref[tap : tap + 1, :]
            high, low = split_bf16(moved)
            lhs[tap * 128 : (tap + 1) * 128, 0:512] = high
            lhs[tap * 128 : (tap + 1) * 128, 512:1024] = low

    fill(range(0, 3))
    x_copy.wait()
    for image in range(2):
        for block in range(4):
            piece = x_in[pl.ds(block * 2 + image, AREA, stride=8), :]
            piece = jnp.concatenate([piece, jnp.zeros((256 - AREA, 128), jnp.float32)], axis=0)
            high, low = split_bf16(piece)
            cols = slice(block * 128, (block + 1) * 128)
            x_hl[image * 256 : (image + 1) * 256, cols] = high
            x_hl[512 + image * 256 : 512 + (image + 1) * 256, cols] = low
    x_high = x_hl[0:512, :]
    x_low = x_hl[512:1024, :]
    copies = []
    for group, out in enumerate((out_a, out_b, out_c)):
        if group < 2:
            fill(range(group * 3 + 3, group * 3 + 6))
        rows = slice(group * 384, group * 384 + 384)
        acc = jnp.dot(lhs[rows, 0:512], x_high, preferred_element_type=jnp.float32)
        acc = acc + jnp.dot(lhs[rows, 512:1024], x_high, preferred_element_type=jnp.float32)
        acc = acc + jnp.dot(lhs[rows, 0:512], x_low, preferred_element_type=jnp.float32)
        for sub in range(3):
            for odd in range(2):
                for spot in range(8):
                    chunk = (spot // 2) * 16 + spot % 2
                    top = sub * 128 + odd * 64 + spot * 8
                    for block in range(4):
                        out[pl.ds(chunk * 24 + sub * 8 + block * 2 + odd, 8, stride=48), :] = acc[
                            top : top + 8, block * 128 : (block + 1) * 128
                        ]
        copy = pltpu.make_async_copy(
            out.reshape(64, 24, 128), out_hbm.at[:, pl.ds(group * 24, 24), :], out_sem.at[group]
        )
        copy.start()
        copies.append(copy)
    for copy in copies:
        copy.wait()


VM = pl.BlockSpec(memory_space=pltpu.VMEM)


ANY = pl.BlockSpec(memory_space=pl.ANY)


def call_grads(x_rows, d_rows):
    return pl.pallas_call(
        grads_kernel,
        out_shape=jax.ShapeDtypeStruct((64, 72, 128), jnp.float32),
        in_specs=[ANY, ANY, ANY],
        out_specs=ANY,
        scratch_shapes=[
            pltpu.VMEM((AREA * 8, 128), jnp.float32),
            pltpu.VMEM((AREA * 2, 128), jnp.float32),
            pltpu.VMEM((16, 512), jnp.float32),
            pltpu.VMEM((1024, 512), jnp.bfloat16),
            pltpu.VMEM((512, 128), jnp.float32),
            pltpu.VMEM((512, 128), jnp.float32),
            pltpu.VMEM((1152, 1024), jnp.bfloat16),
            pltpu.VMEM((1536, 128), jnp.float32),
            pltpu.VMEM((1536, 128), jnp.float32),
            pltpu.VMEM((1536, 128), jnp.float32),
            pltpu.SemaphoreType.DMA((3,)),
            pltpu.SemaphoreType.DMA((3,)),
        ],
        name="filter_grads",
        cost_estimate=pl.CostEstimate(
            flops=3 * 2 * 1152 * 512 * 512, bytes_accessed=3500000, transcendentals=0
        ),
    )(x_rows, d_rows, jnp.asarray(lane_masks()))


def input_kernel(d_ref, w_ref, mask_ref, out_ref, d_pad, lhs, w_hl):
    me = lax.axis_index("ch")
    d_pad[...] = jnp.zeros_like(d_pad)
    for image in range(2):
        d_pad[image, 16 : 16 + AREA, :] = d_ref[pl.ds(image, AREA, stride=2), :]
    for tap, (row, col) in enumerate(TAPS):
        shift = (row - 1) * SIDE + (col - 1)
        for image in range(2):
            moved = d_pad[image, 16 - shift : 216 - shift, :]
            if col == 0:
                moved = moved * mask_ref[0]
            if col == 2:
                moved = moved * mask_ref[1]
            high, low = split_bf16(moved)
            rows = slice(image * 208, image * 208 + 200)
            lhs[rows, tap * 128 : (tap + 1) * 128] = high
            lhs[rows, 1152 + tap * 128 : 1152 + (tap + 1) * 128] = low
    high, low = split_bf16(w_ref[...])
    w_hl[0] = high
    w_hl[1] = low
    lane = lax.broadcasted_iota(jnp.int32, (AREA, 128), 1)
    for pair in range(2):
        cols = slice(pair * 256, (pair + 1) * 256)
        acc = jnp.dot(lhs[:, 0:1152], w_hl[0, :, cols], preferred_element_type=jnp.float32)
        acc = acc + jnp.dot(lhs[:, 1152:2304], w_hl[0, :, cols], preferred_element_type=jnp.float32)
        acc = acc + jnp.dot(lhs[:, 0:1152], w_hl[1, :, cols], preferred_element_type=jnp.float32)
        for sub in range(2):
            first = acc[0:AREA, sub * 128 : (sub + 1) * 128]
            second = acc[208 : 208 + AREA, sub * 128 : (sub + 1) * 128]
            dest = pair * 4 + sub * 2
            out_ref[(dest + 8 - me) & 7] = jnp.where(lane < 64, first, pltpu.roll(second, 64, 1))
            out_ref[(dest + 9 - me) & 7] = jnp.where(lane < 64, pltpu.roll(first, 64, 1), second)


def call_input(d_rows, w_rows):
    return pl.pallas_call(
        input_kernel,
        out_shape=jax.ShapeDtypeStruct((8, AREA, 128), jnp.float32),
        in_specs=[VM, VM, VM],
        out_specs=VM,
        scratch_shapes=[
            pltpu.VMEM((2, 240, 128), jnp.float32),
            pltpu.VMEM((416, 2304), jnp.bfloat16),
            pltpu.VMEM((2, 1152, 512), jnp.bfloat16),
        ],
        name="input_grads",
        compiler_params=pltpu.CompilerParams(vmem_limit_bytes=20 * 1024 * 1024),
        cost_estimate=pl.CostEstimate(flops=3 * 2 * 416 * 1152 * 512, bytes_accessed=3500000, transcendentals=0),
    )(d_rows, w_rows, jnp.asarray(row_masks()))


def fold(value):
    value = value + pltpu.roll(value, 4, 1)
    value = value + pltpu.roll(value, 2, 1)
    return jnp.sum(value, axis=2, keepdims=True)


def pair_weights(cross, left_sq, right_sq):
    count = len(cross)
    sums = fold(jnp.stack(cross + left_sq + right_sq, axis=0))
    cross, left_sq, right_sq = sums[:count], sums[count : 2 * count], sums[2 * count :]
    left_w = 1.0 - cross / (2.0 * (left_sq + EPSILON))
    right_w = 1.0 - cross / (2.0 * (right_sq + EPSILON))
    return left_w, right_w


def chunk_of(replica):
    return (replica // 2 % 4) * 16 + (replica // 8) * 2 + replica % 2


def tree_kernel(v_ref, out_ref, norm_ref, work):
    half = 32
    cross, left_sq, right_sq = [], [], []
    for index in range(half):
        left, right = v_ref[chunk_of(index)], v_ref[chunk_of(index + half)]
        cross.append(jnp.sum(left * right, axis=0))
        left_sq.append(jnp.sum(left * left, axis=0))
        right_sq.append(jnp.sum(right * right, axis=0))
    first = True
    while half > 1:
        left_w, right_w = pair_weights(cross, left_sq, right_sq)
        cross, left_sq, right_sq = [], [], []
        quarter = half // 2
        for index in range(quarter):
            made = []
            for place in (index, index + quarter):
                if first:
                    left, right = v_ref[chunk_of(place)], v_ref[chunk_of(place + half)]
                else:
                    left, right = work[place], work[place + half]
                value = left_w[place] * left + right_w[place] * right
                work[place] = value
                made.append(value)
            left, right = made
            cross.append(jnp.sum(left * right, axis=0))
            left_sq.append(jnp.sum(left * left, axis=0))
            right_sq.append(jnp.sum(right * right, axis=0))
        first = False
        half = quarter
    left_w, right_w = pair_weights(cross, left_sq, right_sq)
    last = left_w[0] * work[0] + right_w[0] * work[1]
    out_ref[0] = last
    norm = jnp.sum(last * last, axis=0)
    norm = jnp.sum(jnp.sum(norm, axis=1, keepdims=True), axis=0, keepdims=True)
    norm_ref[...] = jnp.broadcast_to(norm[None], norm_ref.shape)


def call_tree(vectors):
    return pl.pallas_call(
        tree_kernel,
        out_shape=(
            jax.ShapeDtypeStruct((1, 9, 8, 128), jnp.float32),
            jax.ShapeDtypeStruct((64, 1, 128), jnp.float32),
        ),
        in_specs=[VM],
        out_specs=(VM, VM),
        scratch_shapes=[pltpu.VMEM((32, 9, 8, 128), jnp.float32)],
        name="pair_tree",
        compiler_params=pltpu.CompilerParams(vmem_limit_bytes=10 * 1024 * 1024),
        cost_estimate=pl.CostEstimate(flops=64 * 9216 * 9, bytes_accessed=2400000, transcendentals=0),
    )(vectors)


def update_kernel(terms_ref, combined_ref, weight_ref, momentum_ref, weight_out, momentum_out):
    norm_sq = jnp.sum(terms_ref[...], axis=0)
    clip_scale = jnp.minimum(
        1.0, 0.5 * math.sqrt(CO * 9 * CI) / jnp.sqrt(norm_sq + EPSILON)
    )
    scale = jnp.broadcast_to(clip_scale, (8, 128))[None]
    new_momentum = MOMENTUM_RATE * momentum_ref[...] + scale * combined_ref[...]
    momentum_out[...] = new_momentum
    weight_out[...] = weight_ref[...] - LEARN_RATE * new_momentum


def call_update(terms, combined, weight, momentum):
    return pl.pallas_call(
        update_kernel,
        out_shape=(jax.ShapeDtypeStruct((9, 8, 128), jnp.float32),) * 2,
        in_specs=[VM] * 4,
        out_specs=(VM, VM),
        name="update",
        compiler_params=pltpu.CompilerParams(vmem_limit_bytes=2 * 1024 * 1024),
    )(terms, combined, weight, momentum)


def norm_terms(spread):
    spread = lax.all_to_all(spread, REP, 0, 0, tiled=True)
    value = jnp.sum(spread, axis=0, keepdims=True)
    planes = lax.axis_size("ch")
    spread = jnp.broadcast_to(value, (planes, 1, 128))
    return lax.all_to_all(spread, "ch", 0, 0, tiled=True)


def own_rows(value):
    return value.transpose(1, 2, 0, 3).reshape(9, 2, 4, 128).transpose(0, 2, 1, 3).reshape(9, 8, 128)


def whole_rows(value):
    return value.reshape(9, 4, 2, 128).transpose(0, 2, 1, 3).reshape(3, 3, 2, 512).transpose(2, 0, 1, 3)


def local(inputs, grad_out, weight, momentum):
    images, height, across, chan_in = inputs.shape
    chan_out = grad_out.shape[3]
    replicas = lax.axis_size(REP)
    planes = lax.axis_size("ch")
    col_count = chan_in // planes
    own_count = chan_out // replicas
    rep_index = lax.axis_index(REP)
    x_rows = (
        inputs.transpose(1, 2, 0, 3)
        .reshape(AREA, images, 4, 128)
        .transpose(0, 2, 1, 3)
        .reshape(AREA * 8, 128)
    )
    d_rows = grad_out.transpose(1, 2, 0, 3).reshape(AREA * images, chan_out)
    w_rows = weight.transpose(1, 2, 0, 3).reshape(9 * chan_out, chan_in)
    sent = call_grads(x_rows, d_rows).reshape(replicas, 9, 8, 128)
    d_later, sent_held = lax.optimization_barrier((d_rows, sent))
    vectors = lax.all_to_all(sent_held, ("x", "y", "core"), 0, 0, tiled=True)
    parts = call_input(d_later, w_rows)
    total = parts[0]
    for step in (4, 3, 5, 2, 6, 1, 7):
        pairs = [(source, (source + step) % planes) for source in range(planes)]
        total = total + lax.ppermute(parts[step], "ch", pairs)
    input_grad = (
        total
        .reshape(height, across, images, col_count)
        .transpose(2, 0, 1, 3)
    )

    owned_w = lax.dynamic_slice_in_dim(weight, rep_index * own_count, own_count, 0)
    vectors, input_grad, owned_w = lax.optimization_barrier((vectors, input_grad, owned_w))
    combined, spread = call_tree(vectors)
    terms = norm_terms(spread)
    new_weight, new_momentum = call_update(
        terms, combined[0], own_rows(owned_w), own_rows(momentum)
    )
    new_weight, new_momentum = whole_rows(new_weight), whole_rows(new_momentum)
    return (input_grad, new_weight, new_momentum)


def solution(mesh):
    devices = mesh.devices.reshape(8, 4, 2, 8)
    split = jax.sharding.Mesh(devices, REP + ("ch",))
    in_specs = (
        P(REP, None, None, None),
        P(REP, None, None, "ch"),
        P("ch", None, None, None),
        P(("ch",) + REP, None, None, None),
    )
    out_specs = (
        P(REP, None, None, "ch"),
        P(("ch",) + REP, None, None, None),
        P(("ch",) + REP, None, None, None),
    )
    return jax.shard_map(local, mesh=split, in_specs=in_specs, out_specs=out_specs, check_vma=False)
```

```python
import math

import jax
import jax.numpy as jnp
import numpy as np
from jax import lax
from jax.experimental import pallas as pl
from jax.experimental.pallas import tpu as pltpu
from jax.sharding import PartitionSpec as P

CO = 1024
CI = 512
EPSILON = 1e-06
MOMENTUM_RATE = 0.9
LEARN_RATE = 0.05
SIDE = 14
REP = ("y", "x", "core")
AREA = SIDE * SIDE
TAPS = [(row, col) for row in range(3) for col in range(3)]


def split_bf16(value):
    high = value.astype(jnp.bfloat16)
    low = (value - high.astype(jnp.float32)).astype(jnp.bfloat16)
    return high, low


def lane_masks():
    masks = np.zeros((16, 512), np.float32)
    for tap, (row, col) in enumerate(TAPS):
        for image in range(2):
            for pos in range(AREA):
                high, wide = pos // SIDE - (row - 1), pos % SIDE - (col - 1)
                if 0 <= high < SIDE and 0 <= wide < SIDE:
                    masks[tap, image * 256 + pos] = 1.0
    return masks


def row_masks():
    masks = np.zeros((2, 200, 128), np.float32)
    pos = np.arange(AREA) % SIDE
    masks[0, :AREA] = (pos + 1 < SIDE)[:, None]
    masks[1, :AREA] = (pos - 1 >= 0)[:, None]
    return masks


def grads_kernel(x_hbm, d_hbm, mask_hbm, out_hbm, x_in, d_in, mask_ref, x_hl, d_pad, d_t, lhs, out_a, out_b, out_c, in_sem, out_sem):
    d_copy = pltpu.make_async_copy(d_hbm, d_in, in_sem.at[0])
    x_copy = pltpu.make_async_copy(x_hbm, x_in, in_sem.at[1])
    mask_copy = pltpu.make_async_copy(mask_hbm, mask_ref, in_sem.at[2])
    d_copy.start()
    mask_copy.start()
    x_copy.start()
    d_pad[...] = jnp.zeros_like(d_pad)
    d_copy.wait()
    for image in range(2):
        d_pad[pl.ds(image * 256, AREA), :] = d_in[pl.ds(image, AREA, stride=2), :]
    for part in range(4):
        d_t[part * 128 : (part + 1) * 128, :] = d_pad[part * 128 : (part + 1) * 128, :].T
    halves = []
    for odd in range(2):
        halves.append(
            jnp.concatenate(
                [d_t[pl.ds(part * 128 + odd, 64, stride=2), :] for part in range(4)], axis=1
            )
        )
    base = jnp.concatenate(halves, axis=0)
    mask_copy.wait()

    def fill(taps):
        for tap in taps:
            row, col = TAPS[tap]
            shift = (row - 1) * SIDE + (col - 1)
            moved = base
            if shift:
                moved = jnp.concatenate(
                    [
                        pltpu.roll(base[:, image * 256 : (image + 1) * 256], shift % 256, 1)
                        for image in range(2)
                    ],
                    axis=1,
                )
                moved = moved * mask_ref[tap : tap + 1, :]
            high, low = split_bf16(moved)
            lhs[tap * 128 : (tap + 1) * 128, 0:512] = high
            lhs[tap * 128 : (tap + 1) * 128, 512:1024] = low

    fill(range(0, 3))
    x_copy.wait()
    for image in range(2):
        for block in range(4):
            piece = x_in[pl.ds(block * 2 + image, AREA, stride=8), :]
            piece = jnp.concatenate([piece, jnp.zeros((256 - AREA, 128), jnp.float32)], axis=0)
            high, low = split_bf16(piece)
            cols = slice(block * 128, (block + 1) * 128)
            x_hl[image * 256 : (image + 1) * 256, cols] = high
            x_hl[512 + image * 256 : 512 + (image + 1) * 256, cols] = low
    copies = []
    for group, out in enumerate((out_a, out_b, out_c)):
        if group < 2:
            fill(range(group * 3 + 3, group * 3 + 6))
        rows = slice(group * 384, group * 384 + 384)
        acc = jnp.dot(lhs[rows, 0:256], x_hl[0:256, :], preferred_element_type=jnp.float32)
        acc = acc + jnp.dot(lhs[rows, 512:768], x_hl[0:256, :], preferred_element_type=jnp.float32)
        acc = acc + jnp.dot(lhs[rows, 0:256], x_hl[512:768, :], preferred_element_type=jnp.float32)
        acc = acc + jnp.dot(lhs[rows, 256:512], x_hl[256:512, :], preferred_element_type=jnp.float32)
        acc = acc + jnp.dot(lhs[rows, 768:1024], x_hl[256:512, :], preferred_element_type=jnp.float32)
        acc = acc + jnp.dot(lhs[rows, 256:512], x_hl[768:1024, :], preferred_element_type=jnp.float32)
        for sub in range(3):
            for odd in range(2):
                for block in range(4):
                    out[pl.ds(sub * 8 + block * 2 + odd, 64, stride=24), :] = acc[
                        sub * 128 + odd * 64 : sub * 128 + odd * 64 + 64,
                        block * 128 : (block + 1) * 128,
                    ]
        copy = pltpu.make_async_copy(
            out.reshape(64, 24, 128), out_hbm.at[:, pl.ds(group * 24, 24), :], out_sem.at[group]
        )
        copy.start()
        copies.append(copy)
    for copy in copies:
        copy.wait()


VM = pl.BlockSpec(memory_space=pltpu.VMEM)


ANY = pl.BlockSpec(memory_space=pl.ANY)


def call_grads(x_rows, d_rows):
    return pl.pallas_call(
        grads_kernel,
        out_shape=jax.ShapeDtypeStruct((64, 72, 128), jnp.float32),
        in_specs=[ANY, ANY, ANY],
        out_specs=ANY,
        scratch_shapes=[
            pltpu.VMEM((AREA * 8, 128), jnp.float32),
            pltpu.VMEM((AREA * 2, 128), jnp.float32),
            pltpu.VMEM((16, 512), jnp.float32),
            pltpu.VMEM((1024, 512), jnp.bfloat16),
            pltpu.VMEM((512, 128), jnp.float32),
            pltpu.VMEM((512, 128), jnp.float32),
            pltpu.VMEM((1152, 1024), jnp.bfloat16),
            pltpu.VMEM((1536, 128), jnp.float32),
            pltpu.VMEM((1536, 128), jnp.float32),
            pltpu.VMEM((1536, 128), jnp.float32),
            pltpu.SemaphoreType.DMA((3,)),
            pltpu.SemaphoreType.DMA((3,)),
        ],
        name="filter_grads",
        cost_estimate=pl.CostEstimate(
            flops=3 * 2 * 1152 * 512 * 512, bytes_accessed=3500000, transcendentals=0
        ),
    )(x_rows, d_rows, jnp.asarray(lane_masks()))


def input_kernel(d_ref, w_ref, mask_ref, out_ref, d_pad, lhs, w_hl):
    me = lax.axis_index("ch")
    d_pad[...] = jnp.zeros_like(d_pad)
    for image in range(2):
        d_pad[image, 16 : 16 + AREA, :] = d_ref[pl.ds(image, AREA, stride=2), :]
    for tap, (row, col) in enumerate(TAPS):
        shift = (row - 1) * SIDE + (col - 1)
        for image in range(2):
            moved = d_pad[image, 16 - shift : 216 - shift, :]
            if col == 0:
                moved = moved * mask_ref[0]
            if col == 2:
                moved = moved * mask_ref[1]
            high, low = split_bf16(moved)
            rows = slice(image * 208, image * 208 + 200)
            lhs[rows, tap * 128 : (tap + 1) * 128] = high
            lhs[rows, 1152 + tap * 128 : 1152 + (tap + 1) * 128] = low
    high, low = split_bf16(w_ref[...])
    w_hl[0] = high
    w_hl[1] = low
    lane = lax.broadcasted_iota(jnp.int32, (AREA, 128), 1)
    for pair in range(2):
        cols = slice(pair * 256, (pair + 1) * 256)
        acc = jnp.dot(lhs[:, 0:1152], w_hl[0, :, cols], preferred_element_type=jnp.float32)
        acc = acc + jnp.dot(lhs[:, 1152:2304], w_hl[0, :, cols], preferred_element_type=jnp.float32)
        acc = acc + jnp.dot(lhs[:, 0:1152], w_hl[1, :, cols], preferred_element_type=jnp.float32)
        for sub in range(2):
            first = acc[0:AREA, sub * 128 : (sub + 1) * 128]
            second = acc[208 : 208 + AREA, sub * 128 : (sub + 1) * 128]
            dest = pair * 4 + sub * 2
            out_ref[(dest + 8 - me) & 7] = jnp.where(lane < 64, first, pltpu.roll(second, 64, 1))
            out_ref[(dest + 9 - me) & 7] = jnp.where(lane < 64, pltpu.roll(first, 64, 1), second)


def call_input(d_rows, w_rows):
    return pl.pallas_call(
        input_kernel,
        out_shape=jax.ShapeDtypeStruct((8, AREA, 128), jnp.float32),
        in_specs=[VM, VM, VM],
        out_specs=VM,
        scratch_shapes=[
            pltpu.VMEM((2, 240, 128), jnp.float32),
            pltpu.VMEM((416, 2304), jnp.bfloat16),
            pltpu.VMEM((2, 1152, 512), jnp.bfloat16),
        ],
        name="input_grads",
        compiler_params=pltpu.CompilerParams(vmem_limit_bytes=20 * 1024 * 1024),
        cost_estimate=pl.CostEstimate(flops=3 * 2 * 416 * 1152 * 512, bytes_accessed=3500000, transcendentals=0),
    )(d_rows, w_rows, jnp.asarray(row_masks()))


def fold(value):
    value = value + pltpu.roll(value, 4, 1)
    value = value + pltpu.roll(value, 2, 1)
    return jnp.sum(value, axis=2, keepdims=True)


def pair_weights(cross, left_sq, right_sq):
    count = len(cross)
    sums = fold(jnp.stack(cross + left_sq + right_sq, axis=0))
    cross, left_sq, right_sq = sums[:count], sums[count : 2 * count], sums[2 * count :]
    left_w = 1.0 - cross / (2.0 * (left_sq + EPSILON))
    right_w = 1.0 - cross / (2.0 * (right_sq + EPSILON))
    return left_w, right_w


def tree_kernel(v_ref, out_ref, norm_ref, work):
    half = 32
    cross, left_sq, right_sq = [], [], []
    for index in range(half):
        left, right = v_ref[index], v_ref[index + half]
        cross.append(jnp.sum(left * right, axis=0))
        left_sq.append(jnp.sum(left * left, axis=0))
        right_sq.append(jnp.sum(right * right, axis=0))
    src = v_ref
    while half > 1:
        left_w, right_w = pair_weights(cross, left_sq, right_sq)
        cross, left_sq, right_sq = [], [], []
        quarter = half // 2
        for index in range(quarter):
            made = []
            for place in (index, index + quarter):
                value = left_w[place] * src[place] + right_w[place] * src[place + half]
                work[place] = value
                made.append(value)
            left, right = made
            cross.append(jnp.sum(left * right, axis=0))
            left_sq.append(jnp.sum(left * left, axis=0))
            right_sq.append(jnp.sum(right * right, axis=0))
        src = work
        half = quarter
    left_w, right_w = pair_weights(cross, left_sq, right_sq)
    last = left_w[0] * work[0] + right_w[0] * work[1]
    out_ref[0] = last
    norm = jnp.sum(last * last, axis=0)
    norm = jnp.sum(jnp.sum(norm, axis=1, keepdims=True), axis=0, keepdims=True)
    norm_ref[...] = jnp.broadcast_to(norm[None], norm_ref.shape)


def call_tree(vectors):
    return pl.pallas_call(
        tree_kernel,
        out_shape=(
            jax.ShapeDtypeStruct((1, 9, 8, 128), jnp.float32),
            jax.ShapeDtypeStruct((16, 1, 128), jnp.float32),
        ),
        in_specs=[VM],
        out_specs=(VM, VM),
        scratch_shapes=[pltpu.VMEM((32, 9, 8, 128), jnp.float32)],
        name="pair_tree",
        compiler_params=pltpu.CompilerParams(vmem_limit_bytes=10 * 1024 * 1024),
        cost_estimate=pl.CostEstimate(flops=64 * 9216 * 9, bytes_accessed=2400000, transcendentals=0),
    )(vectors)


def update_kernel(terms_ref, combined_ref, weight_ref, momentum_ref, weight_out, momentum_out):
    norm_sq = jnp.sum(terms_ref[...], axis=0)
    clip_scale = jnp.minimum(
        1.0, 0.5 * math.sqrt(CO * 9 * CI) / jnp.sqrt(norm_sq + EPSILON)
    )
    scale = jnp.broadcast_to(clip_scale, (8, 128))[None]
    new_momentum = MOMENTUM_RATE * momentum_ref[...] + scale * combined_ref[...]
    momentum_out[...] = new_momentum
    weight_out[...] = weight_ref[...] - LEARN_RATE * new_momentum


def call_update(terms, combined, weight, momentum):
    return pl.pallas_call(
        update_kernel,
        out_shape=(jax.ShapeDtypeStruct((9, 8, 128), jnp.float32),) * 2,
        in_specs=[VM] * 4,
        out_specs=(VM, VM),
        name="update",
        compiler_params=pltpu.CompilerParams(vmem_limit_bytes=2 * 1024 * 1024),
    )(terms, combined, weight, momentum)


def norm_terms(spread):
    spread = lax.all_to_all(spread, ("core", "ch"), 0, 0, tiled=True)
    value = jnp.sum(spread, axis=0, keepdims=True)
    spread = jnp.broadcast_to(value, (lax.axis_size(("y", "x")), 1, 128))
    return lax.all_to_all(spread, ("y", "x"), 0, 0, tiled=True)


def own_rows(value):
    return value.transpose(1, 2, 0, 3).reshape(9, 2, 4, 128).transpose(0, 2, 1, 3).reshape(9, 8, 128)


def whole_rows(value):
    return value.reshape(9, 4, 2, 128).transpose(0, 2, 1, 3).reshape(3, 3, 2, 512).transpose(2, 0, 1, 3)


def local(inputs, grad_out, weight, momentum):
    images, height, across, chan_in = inputs.shape
    chan_out = grad_out.shape[3]
    replicas = lax.axis_size(REP)
    planes = lax.axis_size("ch")
    col_count = chan_in // planes
    own_count = chan_out // replicas
    rep_index = lax.axis_index(REP)
    x_rows = (
        inputs.transpose(1, 2, 0, 3)
        .reshape(AREA, images, 4, 128)
        .transpose(0, 2, 1, 3)
        .reshape(AREA * 8, 128)
    )
    d_rows = grad_out.transpose(1, 2, 0, 3).reshape(AREA * images, chan_out)
    w_rows = weight.transpose(1, 2, 0, 3).reshape(9 * chan_out, chan_in)
    sent = call_grads(x_rows, d_rows).reshape(replicas, 9, 8, 128)
    d_later, sent_held = lax.optimization_barrier((d_rows, sent))
    vectors = lax.all_to_all(sent_held, REP, 0, 0, tiled=True)
    parts = call_input(d_later, w_rows)
    total = parts[0]
    for step in (4, 3, 5, 2, 6, 1, 7):
        pairs = [(source, (source + step) % planes) for source in range(planes)]
        total = total + lax.ppermute(parts[step], "ch", pairs)
    input_grad = (
        total
        .reshape(height, across, images, col_count)
        .transpose(2, 0, 1, 3)
    )

    owned_w = lax.dynamic_slice_in_dim(weight, rep_index * own_count, own_count, 0)
    vectors, input_grad, owned_w = lax.optimization_barrier((vectors, input_grad, owned_w))
    combined, spread = call_tree(vectors)
    terms = norm_terms(spread)
    new_weight, new_momentum = call_update(
        terms, combined[0], own_rows(owned_w), own_rows(momentum)
    )
    new_weight, new_momentum = whole_rows(new_weight), whole_rows(new_momentum)
    return (input_grad, new_weight, new_momentum)


def solution(mesh):
    devices = mesh.devices.reshape(8, 4, 2, 8)
    split = jax.sharding.Mesh(devices, REP + ("ch",))
    in_specs = (
        P(REP, None, None, None),
        P(REP, None, None, "ch"),
        P("ch", None, None, None),
        P(("ch",) + REP, None, None, None),
    )
    out_specs = (
        P(REP, None, None, "ch"),
        P(("ch",) + REP, None, None, None),
        P(("ch",) + REP, None, None, None),
    )
    return jax.shard_map(local, mesh=split, in_specs=in_specs, out_specs=out_specs, check_vma=False)
```

```python
import math

import jax
import jax.numpy as jnp
import numpy as np
from jax import lax
from jax.experimental import pallas as pl
from jax.experimental.pallas import tpu as pltpu
from jax.sharding import PartitionSpec as P

CO = 1024
CI = 512
EPSILON = 1e-06
MOMENTUM_RATE = 0.9
LEARN_RATE = 0.05
SIDE = 14
HEAD = 36


def chunk_of(replica):
    return {0: HEAD, HEAD: 0}.get(replica, replica)


REP_ORDER = [[chunk_of(place) for place in range(64)]]
CH_ORDER = [[4, 5, 6, 7, 0, 1, 2, 3]]
AREA = SIDE * SIDE
TAPS = [(row, col) for row in range(3) for col in range(3)]


def split_bf16(value):
    high = value.astype(jnp.bfloat16)
    low = (value - high.astype(jnp.float32)).astype(jnp.bfloat16)
    return high, low


def lane_masks():
    masks = np.zeros((16, 512), np.float32)
    for tap, (row, col) in enumerate(TAPS):
        for image in range(2):
            for pos in range(AREA):
                high, wide = pos // SIDE - (row - 1), pos % SIDE - (col - 1)
                if 0 <= high < SIDE and 0 <= wide < SIDE:
                    masks[tap, image * 256 + pos] = 1.0
    return masks


def row_masks():
    masks = np.zeros((2, 200, 128), np.float32)
    pos = np.arange(AREA) % SIDE
    masks[0, :AREA] = (pos + 1 < SIDE)[:, None]
    masks[1, :AREA] = (pos - 1 >= 0)[:, None]
    return masks


def grads_kernel(x_hbm, d_hbm, mask_hbm, out_hbm, x_in, d_in, mask_ref, x_hl, d_pad, d_t, lhs, out_a, out_b, out_c, in_sem, out_sem):
    d_copy = pltpu.make_async_copy(d_hbm, d_in, in_sem.at[0])
    x_copy = pltpu.make_async_copy(x_hbm, x_in, in_sem.at[1])
    mask_copy = pltpu.make_async_copy(mask_hbm, mask_ref, in_sem.at[2])
    d_copy.start()
    mask_copy.start()
    x_copy.start()
    d_pad[...] = jnp.zeros_like(d_pad)
    d_copy.wait()
    for image in range(2):
        d_pad[pl.ds(image * 256, AREA), :] = d_in[pl.ds(image, AREA, stride=2), :]
    for part in range(4):
        d_t[part * 128 : (part + 1) * 128, :] = d_pad[part * 128 : (part + 1) * 128, :].T
    halves = []
    for odd in range(2):
        halves.append(
            jnp.concatenate(
                [d_t[pl.ds(part * 128 + odd, 64, stride=2), :] for part in range(4)], axis=1
            )
        )
    base = jnp.concatenate(halves, axis=0)
    mask_copy.wait()

    def fill(taps):
        for tap in taps:
            row, col = TAPS[tap]
            shift = (row - 1) * SIDE + (col - 1)
            moved = base
            if shift:
                moved = jnp.concatenate(
                    [
                        pltpu.roll(base[:, image * 256 : (image + 1) * 256], shift % 256, 1)
                        for image in range(2)
                    ],
                    axis=1,
                )
                moved = moved * mask_ref[tap : tap + 1, :]
            high, low = split_bf16(moved)
            lhs[tap * 128 : (tap + 1) * 128, 0:512] = high
            lhs[tap * 128 : (tap + 1) * 128, 512:1024] = low

    fill(range(0, 3))
    x_copy.wait()
    for image in range(2):
        for block in range(4):
            piece = x_in[pl.ds(block * 2 + image, AREA, stride=8), :]
            piece = jnp.concatenate([piece, jnp.zeros((256 - AREA, 128), jnp.float32)], axis=0)
            high, low = split_bf16(piece)
            cols = slice(block * 128, (block + 1) * 128)
            x_hl[image * 256 : (image + 1) * 256, cols] = high
            x_hl[512 + image * 256 : 512 + (image + 1) * 256, cols] = low
    copies = []
    for group, out in enumerate((out_a, out_b, out_c)):
        if group < 2:
            fill(range(group * 3 + 3, group * 3 + 6))
        rows = slice(group * 384, group * 384 + 384)
        acc = jnp.dot(lhs[rows, 0:256], x_hl[0:256, :], preferred_element_type=jnp.float32)
        acc = acc + jnp.dot(lhs[rows, 512:768], x_hl[0:256, :], preferred_element_type=jnp.float32)
        acc = acc + jnp.dot(lhs[rows, 0:256], x_hl[512:768, :], preferred_element_type=jnp.float32)
        acc = acc + jnp.dot(lhs[rows, 256:512], x_hl[256:512, :], preferred_element_type=jnp.float32)
        acc = acc + jnp.dot(lhs[rows, 768:1024], x_hl[256:512, :], preferred_element_type=jnp.float32)
        acc = acc + jnp.dot(lhs[rows, 256:512], x_hl[768:1024, :], preferred_element_type=jnp.float32)
        for sub in range(3):
            for odd in range(2):
                for block in range(4):
                    out[pl.ds(sub * 8 + block * 2 + odd, 64, stride=24), :] = acc[
                        sub * 128 + odd * 64 : sub * 128 + odd * 64 + 64,
                        block * 128 : (block + 1) * 128,
                    ]
        chunks = out.reshape(64, 24, 128)
        runs = ((0, HEAD, 1), (1, 1, HEAD - 1), (HEAD, 0, 1), (HEAD + 1, HEAD + 1, 63 - HEAD))
        for part, (source, target, count) in enumerate(runs):
            copy = pltpu.make_async_copy(
                chunks.at[pl.ds(source, count)],
                out_hbm.at[pl.ds(target, count), pl.ds(group * 24, 24), :],
                out_sem.at[group * 4 + part],
            )
            copy.start()
            copies.append(copy)
    for copy in copies:
        copy.wait()


VM = pl.BlockSpec(memory_space=pltpu.VMEM)


ANY = pl.BlockSpec(memory_space=pl.ANY)


def call_grads(x_rows, d_rows):
    return pl.pallas_call(
        grads_kernel,
        out_shape=jax.ShapeDtypeStruct((64, 72, 128), jnp.float32),
        in_specs=[ANY, ANY, ANY],
        out_specs=ANY,
        scratch_shapes=[
            pltpu.VMEM((AREA * 8, 128), jnp.float32),
            pltpu.VMEM((AREA * 2, 128), jnp.float32),
            pltpu.VMEM((16, 512), jnp.float32),
            pltpu.VMEM((1024, 512), jnp.bfloat16),
            pltpu.VMEM((512, 128), jnp.float32),
            pltpu.VMEM((512, 128), jnp.float32),
            pltpu.VMEM((1152, 1024), jnp.bfloat16),
            pltpu.VMEM((1536, 128), jnp.float32),
            pltpu.VMEM((1536, 128), jnp.float32),
            pltpu.VMEM((1536, 128), jnp.float32),
            pltpu.SemaphoreType.DMA((3,)),
            pltpu.SemaphoreType.DMA((12,)),
        ],
        name="filter_grads",
        cost_estimate=pl.CostEstimate(
            flops=3 * 2 * 1152 * 512 * 512, bytes_accessed=3500000, transcendentals=0
        ),
    )(x_rows, d_rows, jnp.asarray(lane_masks()))


def input_kernel(d_ref, w_ref, mask_ref, out_ref, d_pad, lhs, w_hl):
    me = lax.axis_index("ch")
    d_pad[...] = jnp.zeros_like(d_pad)
    for image in range(2):
        d_pad[image, 16 : 16 + AREA, :] = d_ref[pl.ds(image, AREA, stride=2), :]
    for tap, (row, col) in enumerate(TAPS):
        shift = (row - 1) * SIDE + (col - 1)
        for image in range(2):
            moved = d_pad[image, 16 - shift : 216 - shift, :]
            if col == 0:
                moved = moved * mask_ref[0]
            if col == 2:
                moved = moved * mask_ref[1]
            high, low = split_bf16(moved)
            rows = slice(image * 208, image * 208 + 200)
            lhs[rows, tap * 128 : (tap + 1) * 128] = high
            lhs[rows, 1152 + tap * 128 : 1152 + (tap + 1) * 128] = low
    high, low = split_bf16(w_ref[...])
    w_hl[0] = high
    w_hl[1] = low
    lane = lax.broadcasted_iota(jnp.int32, (AREA, 128), 1)
    for pair in range(2):
        cols = slice(pair * 256, (pair + 1) * 256)
        acc = jnp.dot(lhs[:, 0:1152], w_hl[0, :, cols], preferred_element_type=jnp.float32)
        acc = acc + jnp.dot(lhs[:, 1152:2304], w_hl[0, :, cols], preferred_element_type=jnp.float32)
        acc = acc + jnp.dot(lhs[:, 0:1152], w_hl[1, :, cols], preferred_element_type=jnp.float32)
        for sub in range(2):
            first = acc[0:AREA, sub * 128 : (sub + 1) * 128]
            second = acc[208 : 208 + AREA, sub * 128 : (sub + 1) * 128]
            dest = pair * 4 + sub * 2
            out_ref[(dest + 8 - me) & 7] = jnp.where(lane < 64, first, pltpu.roll(second, 64, 1))
            out_ref[(dest + 9 - me) & 7] = jnp.where(lane < 64, pltpu.roll(first, 64, 1), second)


def call_input(d_rows, w_rows):
    return pl.pallas_call(
        input_kernel,
        out_shape=jax.ShapeDtypeStruct((8, AREA, 128), jnp.float32),
        in_specs=[VM, VM, VM],
        out_specs=VM,
        scratch_shapes=[
            pltpu.VMEM((2, 240, 128), jnp.float32),
            pltpu.VMEM((416, 2304), jnp.bfloat16),
            pltpu.VMEM((2, 1152, 512), jnp.bfloat16),
        ],
        name="input_grads",
        compiler_params=pltpu.CompilerParams(vmem_limit_bytes=20 * 1024 * 1024),
        cost_estimate=pl.CostEstimate(flops=3 * 2 * 416 * 1152 * 512, bytes_accessed=3500000, transcendentals=0),
    )(d_rows, w_rows, jnp.asarray(row_masks()))


def fold(value):
    value = value + pltpu.roll(value, 4, 1)
    value = value + pltpu.roll(value, 2, 1)
    return jnp.sum(value, axis=2, keepdims=True)


def pair_weights(cross, left_sq, right_sq):
    count = len(cross)
    sums = fold(jnp.stack(cross + left_sq + right_sq, axis=0))
    cross, left_sq, right_sq = sums[:count], sums[count : 2 * count], sums[2 * count :]
    left_w = 1.0 - cross / (2.0 * (left_sq + EPSILON))
    right_w = 1.0 - cross / (2.0 * (right_sq + EPSILON))
    return left_w, right_w


def tree_kernel(v_ref, out_ref, norm_ref, work):
    half = 32
    cross, left_sq, right_sq = [], [], []
    for index in range(half):
        left, right = v_ref[chunk_of(index)], v_ref[chunk_of(index + half)]
        cross.append(jnp.sum(left * right, axis=0))
        left_sq.append(jnp.sum(left * left, axis=0))
        right_sq.append(jnp.sum(right * right, axis=0))
    first = True
    while half > 1:
        left_w, right_w = pair_weights(cross, left_sq, right_sq)
        cross, left_sq, right_sq = [], [], []
        quarter = half // 2
        for index in range(quarter):
            made = []
            for place in (index, index + quarter):
                if first:
                    left, right = v_ref[chunk_of(place)], v_ref[chunk_of(place + half)]
                else:
                    left, right = work[place], work[place + half]
                value = left_w[place] * left + right_w[place] * right
                work[place] = value
                made.append(value)
            left, right = made
            cross.append(jnp.sum(left * right, axis=0))
            left_sq.append(jnp.sum(left * left, axis=0))
            right_sq.append(jnp.sum(right * right, axis=0))
        first = False
        half = quarter
    left_w, right_w = pair_weights(cross, left_sq, right_sq)
    last = left_w[0] * work[0] + right_w[0] * work[1]
    out_ref[0] = last
    norm = jnp.sum(last * last, axis=0)
    norm = jnp.sum(jnp.sum(norm, axis=1, keepdims=True), axis=0, keepdims=True)
    norm_ref[...] = jnp.broadcast_to(norm[None], norm_ref.shape)


def call_tree(vectors):
    return pl.pallas_call(
        tree_kernel,
        out_shape=(
            jax.ShapeDtypeStruct((1, 9, 8, 128), jnp.float32),
            jax.ShapeDtypeStruct((64, 1, 128), jnp.float32),
        ),
        in_specs=[VM],
        out_specs=(VM, VM),
        scratch_shapes=[pltpu.VMEM((32, 9, 8, 128), jnp.float32)],
        name="pair_tree",
        compiler_params=pltpu.CompilerParams(vmem_limit_bytes=10 * 1024 * 1024),
        cost_estimate=pl.CostEstimate(flops=64 * 9216 * 9, bytes_accessed=2400000, transcendentals=0),
    )(vectors)


def update_kernel(terms_ref, combined_ref, weight_ref, momentum_ref, weight_out, momentum_out):
    norm_sq = jnp.sum(terms_ref[...], axis=0)
    clip_scale = jnp.minimum(
        1.0, 0.5 * math.sqrt(CO * 9 * CI) / jnp.sqrt(norm_sq + EPSILON)
    )
    scale = jnp.broadcast_to(clip_scale, (8, 128))[None]
    new_momentum = MOMENTUM_RATE * momentum_ref[...] + scale * combined_ref[...]
    momentum_out[...] = new_momentum
    weight_out[...] = weight_ref[...] - LEARN_RATE * new_momentum


def call_update(terms, combined, weight, momentum):
    return pl.pallas_call(
        update_kernel,
        out_shape=(jax.ShapeDtypeStruct((9, 8, 128), jnp.float32),) * 2,
        in_specs=[VM] * 4,
        out_specs=(VM, VM),
        name="update",
        compiler_params=pltpu.CompilerParams(vmem_limit_bytes=2 * 1024 * 1024),
    )(terms, combined, weight, momentum)


def norm_terms(spread):
    spread = lax.all_to_all(spread, "rep", 0, 0, tiled=True, axis_index_groups=REP_ORDER)
    value = jnp.sum(spread, axis=0, keepdims=True)
    spread = jnp.broadcast_to(value, (lax.axis_size("ch"), 1, 128))
    return lax.all_to_all(spread, "ch", 0, 0, tiled=True, axis_index_groups=CH_ORDER)


def own_rows(value):
    return value.transpose(1, 2, 0, 3).reshape(9, 2, 4, 128).transpose(0, 2, 1, 3).reshape(9, 8, 128)


def whole_rows(value):
    return value.reshape(9, 4, 2, 128).transpose(0, 2, 1, 3).reshape(3, 3, 2, 512).transpose(2, 0, 1, 3)


def local(inputs, grad_out, weight, momentum):
    images, height, across, chan_in = inputs.shape
    chan_out = grad_out.shape[3]
    replicas = lax.axis_size("rep")
    planes = lax.axis_size("ch")
    col_count = chan_in // planes
    own_count = chan_out // replicas
    rep_index = lax.axis_index("rep")
    x_rows = (
        inputs.transpose(1, 2, 0, 3)
        .reshape(AREA, images, 4, 128)
        .transpose(0, 2, 1, 3)
        .reshape(AREA * 8, 128)
    )
    d_rows = grad_out.transpose(1, 2, 0, 3).reshape(AREA * images, chan_out)
    w_rows = weight.transpose(1, 2, 0, 3).reshape(9 * chan_out, chan_in)
    sent = call_grads(x_rows, d_rows).reshape(replicas, 9, 8, 128)
    d_later, sent_held = lax.optimization_barrier((d_rows, sent))
    vectors = lax.all_to_all(
        sent_held, "rep", 0, 0, tiled=True, axis_index_groups=REP_ORDER
    )
    parts = call_input(d_later, w_rows)
    total = parts[0]
    for step in (4, 3, 5, 2, 6, 1, 7):
        pairs = [(source, (source + step) % planes) for source in range(planes)]
        total = total + lax.ppermute(parts[step], "ch", pairs)
    input_grad = (
        total
        .reshape(height, across, images, col_count)
        .transpose(2, 0, 1, 3)
    )

    owned_w = lax.dynamic_slice_in_dim(weight, rep_index * own_count, own_count, 0)
    vectors, input_grad, owned_w = lax.optimization_barrier((vectors, input_grad, owned_w))
    combined, spread = call_tree(vectors)
    terms = norm_terms(spread)
    new_weight, new_momentum = call_update(
        terms, combined[0], own_rows(owned_w), own_rows(momentum)
    )
    new_weight, new_momentum = whole_rows(new_weight), whole_rows(new_momentum)
    return (input_grad, new_weight, new_momentum)


def solution(mesh):
    in_specs = (
        P("rep", None, None, None),
        P("rep", None, None, "ch"),
        P("ch", None, None, None),
        P(("ch", "rep"), None, None, None),
    )
    out_specs = (
        P("rep", None, None, "ch"),
        P(("ch", "rep"), None, None, None),
        P(("ch", "rep"), None, None, None),
    )
    return jax.shard_map(local, mesh=mesh, in_specs=in_specs, out_specs=out_specs, check_vma=False)
```

```python
import math

import jax
import jax.numpy as jnp
import numpy as np
from jax import lax
from jax.experimental import pallas as pl
from jax.experimental.pallas import tpu as pltpu
from jax.sharding import PartitionSpec as P

CO = 1024
CI = 512
EPSILON = 1e-06
MOMENTUM_RATE = 0.9
LEARN_RATE = 0.05
SIDE = 14
HEAD = 37
REP = ("y", "x", "core")


def chunk_of(replica):
    return {0: HEAD, HEAD: 0}.get(replica, replica)


REP_ORDER = [[chunk_of(place) for place in range(64)]]
CROSS_ORDER = [[(place + 4) % 16 for place in range(16)]]
PLANE_ORDER = [[(place + 18) % 32 for place in range(32)]]
AREA = SIDE * SIDE
TAPS = [(row, col) for row in range(3) for col in range(3)]


def split_bf16(value):
    high = value.astype(jnp.bfloat16)
    low = (value - high.astype(jnp.float32)).astype(jnp.bfloat16)
    return high, low


def lane_masks():
    masks = np.zeros((16, 512), np.float32)
    for tap, (row, col) in enumerate(TAPS):
        for image in range(2):
            for pos in range(AREA):
                high, wide = pos // SIDE - (row - 1), pos % SIDE - (col - 1)
                if 0 <= high < SIDE and 0 <= wide < SIDE:
                    masks[tap, image * 256 + pos] = 1.0
    return masks


def row_masks():
    masks = np.zeros((2, 200, 128), np.float32)
    pos = np.arange(AREA) % SIDE
    masks[0, :AREA] = (pos + 1 < SIDE)[:, None]
    masks[1, :AREA] = (pos - 1 >= 0)[:, None]
    return masks


def grads_kernel(x_hbm, d_hbm, mask_hbm, out_hbm, x_in, d_in, mask_ref, x_hl, d_pad, d_t, lhs, out_a, out_b, out_c, in_sem, out_sem):
    d_copy = pltpu.make_async_copy(d_hbm, d_in, in_sem.at[0])
    x_copy = pltpu.make_async_copy(x_hbm, x_in, in_sem.at[1])
    mask_copy = pltpu.make_async_copy(mask_hbm, mask_ref, in_sem.at[2])
    d_copy.start()
    mask_copy.start()
    x_copy.start()
    d_pad[...] = jnp.zeros_like(d_pad)
    d_copy.wait()
    for image in range(2):
        d_pad[pl.ds(image * 256, AREA), :] = d_in[pl.ds(image, AREA, stride=2), :]
    for part in range(4):
        d_t[part * 128 : (part + 1) * 128, :] = d_pad[part * 128 : (part + 1) * 128, :].T
    halves = []
    for odd in range(2):
        halves.append(
            jnp.concatenate(
                [d_t[pl.ds(part * 128 + odd, 64, stride=2), :] for part in range(4)], axis=1
            )
        )
    base = jnp.concatenate(halves, axis=0)
    mask_copy.wait()

    def fill(taps):
        for tap in taps:
            row, col = TAPS[tap]
            shift = (row - 1) * SIDE + (col - 1)
            moved = base
            if shift:
                moved = jnp.concatenate(
                    [
                        pltpu.roll(base[:, image * 256 : (image + 1) * 256], shift % 256, 1)
                        for image in range(2)
                    ],
                    axis=1,
                )
                moved = moved * mask_ref[tap : tap + 1, :]
            high, low = split_bf16(moved)
            lhs[tap * 128 : (tap + 1) * 128, 0:512] = high
            lhs[tap * 128 : (tap + 1) * 128, 512:1024] = low

    fill(range(0, 3))
    x_copy.wait()
    for image in range(2):
        for block in range(4):
            piece = x_in[pl.ds(block * 2 + image, AREA, stride=8), :]
            piece = jnp.concatenate([piece, jnp.zeros((256 - AREA, 128), jnp.float32)], axis=0)
            high, low = split_bf16(piece)
            cols = slice(block * 128, (block + 1) * 128)
            x_hl[image * 256 : (image + 1) * 256, cols] = high
            x_hl[512 + image * 256 : 512 + (image + 1) * 256, cols] = low
    copies = []
    for group, out in enumerate((out_a, out_b, out_c)):
        if group < 2:
            fill(range(group * 3 + 3, group * 3 + 6))
        rows = slice(group * 384, group * 384 + 384)
        acc = jnp.dot(lhs[rows, 0:256], x_hl[0:256, :], preferred_element_type=jnp.float32)
        acc = acc + jnp.dot(lhs[rows, 512:768], x_hl[0:256, :], preferred_element_type=jnp.float32)
        acc = acc + jnp.dot(lhs[rows, 0:256], x_hl[512:768, :], preferred_element_type=jnp.float32)
        acc = acc + jnp.dot(lhs[rows, 256:512], x_hl[256:512, :], preferred_element_type=jnp.float32)
        acc = acc + jnp.dot(lhs[rows, 768:1024], x_hl[256:512, :], preferred_element_type=jnp.float32)
        acc = acc + jnp.dot(lhs[rows, 256:512], x_hl[768:1024, :], preferred_element_type=jnp.float32)
        for sub in range(3):
            for odd in range(2):
                for block in range(4):
                    out[pl.ds(sub * 8 + block * 2 + odd, 64, stride=24), :] = acc[
                        sub * 128 + odd * 64 : sub * 128 + odd * 64 + 64,
                        block * 128 : (block + 1) * 128,
                    ]
        chunks = out.reshape(64, 24, 128)
        runs = ((0, HEAD, 1), (1, 1, HEAD - 1), (HEAD, 0, 1), (HEAD + 1, HEAD + 1, 63 - HEAD))
        for part, (source, target, count) in enumerate(runs):
            copy = pltpu.make_async_copy(
                chunks.at[pl.ds(source, count)],
                out_hbm.at[pl.ds(target, count), pl.ds(group * 24, 24), :],
                out_sem.at[group * 4 + part],
            )
            copy.start()
            copies.append(copy)
    for copy in copies:
        copy.wait()


VM = pl.BlockSpec(memory_space=pltpu.VMEM)


ANY = pl.BlockSpec(memory_space=pl.ANY)


def call_grads(x_rows, d_rows):
    return pl.pallas_call(
        grads_kernel,
        out_shape=jax.ShapeDtypeStruct((64, 72, 128), jnp.float32),
        in_specs=[ANY, ANY, ANY],
        out_specs=ANY,
        scratch_shapes=[
            pltpu.VMEM((AREA * 8, 128), jnp.float32),
            pltpu.VMEM((AREA * 2, 128), jnp.float32),
            pltpu.VMEM((16, 512), jnp.float32),
            pltpu.VMEM((1024, 512), jnp.bfloat16),
            pltpu.VMEM((512, 128), jnp.float32),
            pltpu.VMEM((512, 128), jnp.float32),
            pltpu.VMEM((1152, 1024), jnp.bfloat16),
            pltpu.VMEM((1536, 128), jnp.float32),
            pltpu.VMEM((1536, 128), jnp.float32),
            pltpu.VMEM((1536, 128), jnp.float32),
            pltpu.SemaphoreType.DMA((3,)),
            pltpu.SemaphoreType.DMA((12,)),
        ],
        name="filter_grads",
        cost_estimate=pl.CostEstimate(
            flops=3 * 2 * 1152 * 512 * 512, bytes_accessed=3500000, transcendentals=0
        ),
    )(x_rows, d_rows, jnp.asarray(lane_masks()))


def input_kernel(d_ref, w_ref, mask_ref, out_ref, d_pad, lhs, w_hl):
    me = lax.axis_index("ch")
    d_pad[...] = jnp.zeros_like(d_pad)
    for image in range(2):
        d_pad[image, 16 : 16 + AREA, :] = d_ref[pl.ds(image, AREA, stride=2), :]
    for tap, (row, col) in enumerate(TAPS):
        shift = (row - 1) * SIDE + (col - 1)
        for image in range(2):
            moved = d_pad[image, 16 - shift : 216 - shift, :]
            if col == 0:
                moved = moved * mask_ref[0]
            if col == 2:
                moved = moved * mask_ref[1]
            high, low = split_bf16(moved)
            rows = slice(image * 208, image * 208 + 200)
            lhs[rows, tap * 128 : (tap + 1) * 128] = high
            lhs[rows, 1152 + tap * 128 : 1152 + (tap + 1) * 128] = low
    high, low = split_bf16(w_ref[...])
    w_hl[0] = high
    w_hl[1] = low
    lane = lax.broadcasted_iota(jnp.int32, (AREA, 128), 1)
    for pair in range(2):
        cols = slice(pair * 256, (pair + 1) * 256)
        acc = jnp.dot(lhs[:, 0:1152], w_hl[0, :, cols], preferred_element_type=jnp.float32)
        acc = acc + jnp.dot(lhs[:, 1152:2304], w_hl[0, :, cols], preferred_element_type=jnp.float32)
        acc = acc + jnp.dot(lhs[:, 0:1152], w_hl[1, :, cols], preferred_element_type=jnp.float32)
        for sub in range(2):
            first = acc[0:AREA, sub * 128 : (sub + 1) * 128]
            second = acc[208 : 208 + AREA, sub * 128 : (sub + 1) * 128]
            dest = pair * 4 + sub * 2
            out_ref[(dest + 8 - me) & 7] = jnp.where(lane < 64, first, pltpu.roll(second, 64, 1))
            out_ref[(dest + 9 - me) & 7] = jnp.where(lane < 64, pltpu.roll(first, 64, 1), second)


def call_input(d_rows, w_rows):
    return pl.pallas_call(
        input_kernel,
        out_shape=jax.ShapeDtypeStruct((8, AREA, 128), jnp.float32),
        in_specs=[VM, VM, VM],
        out_specs=VM,
        scratch_shapes=[
            pltpu.VMEM((2, 240, 128), jnp.float32),
            pltpu.VMEM((416, 2304), jnp.bfloat16),
            pltpu.VMEM((2, 1152, 512), jnp.bfloat16),
        ],
        name="input_grads",
        compiler_params=pltpu.CompilerParams(vmem_limit_bytes=20 * 1024 * 1024),
        cost_estimate=pl.CostEstimate(flops=3 * 2 * 416 * 1152 * 512, bytes_accessed=3500000, transcendentals=0),
    )(d_rows, w_rows, jnp.asarray(row_masks()))


def fold(value):
    value = value + pltpu.roll(value, 4, 1)
    value = value + pltpu.roll(value, 2, 1)
    return jnp.sum(value, axis=2, keepdims=True)


def pair_weights(cross, left_sq, right_sq):
    count = len(cross)
    sums = fold(jnp.stack(cross + left_sq + right_sq, axis=0))
    cross, left_sq, right_sq = sums[:count], sums[count : 2 * count], sums[2 * count :]
    left_w = 1.0 - cross / (2.0 * (left_sq + EPSILON))
    right_w = 1.0 - cross / (2.0 * (right_sq + EPSILON))
    return left_w, right_w


def tree_kernel(v_ref, out_ref, norm_ref, work):
    half = 32
    cross, left_sq, right_sq = [], [], []
    for index in range(half):
        left, right = v_ref[chunk_of(index)], v_ref[chunk_of(index + half)]
        cross.append(jnp.sum(left * right, axis=0))
        left_sq.append(jnp.sum(left * left, axis=0))
        right_sq.append(jnp.sum(right * right, axis=0))
    first = True
    while half > 1:
        left_w, right_w = pair_weights(cross, left_sq, right_sq)
        cross, left_sq, right_sq = [], [], []
        quarter = half // 2
        for index in range(quarter):
            made = []
            for place in (index, index + quarter):
                if first:
                    left, right = v_ref[chunk_of(place)], v_ref[chunk_of(place + half)]
                else:
                    left, right = work[place], work[place + half]
                value = left_w[place] * left + right_w[place] * right
                work[place] = value
                made.append(value)
            left, right = made
            cross.append(jnp.sum(left * right, axis=0))
            left_sq.append(jnp.sum(left * left, axis=0))
            right_sq.append(jnp.sum(right * right, axis=0))
        first = False
        half = quarter
    left_w, right_w = pair_weights(cross, left_sq, right_sq)
    last = left_w[0] * work[0] + right_w[0] * work[1]
    out_ref[0] = last
    norm = jnp.sum(last * last, axis=0)
    norm = jnp.sum(jnp.sum(norm, axis=1, keepdims=True), axis=0, keepdims=True)
    norm_ref[...] = jnp.broadcast_to(norm[None], norm_ref.shape)


def call_tree(vectors):
    return pl.pallas_call(
        tree_kernel,
        out_shape=(
            jax.ShapeDtypeStruct((1, 9, 8, 128), jnp.float32),
            jax.ShapeDtypeStruct((16, 1, 128), jnp.float32),
        ),
        in_specs=[VM],
        out_specs=(VM, VM),
        scratch_shapes=[pltpu.VMEM((32, 9, 8, 128), jnp.float32)],
        name="pair_tree",
        compiler_params=pltpu.CompilerParams(vmem_limit_bytes=10 * 1024 * 1024),
        cost_estimate=pl.CostEstimate(flops=64 * 9216 * 9, bytes_accessed=2400000, transcendentals=0),
    )(vectors)


def update_kernel(terms_ref, combined_ref, weight_ref, momentum_ref, weight_out, momentum_out):
    norm_sq = jnp.sum(terms_ref[...], axis=0)
    clip_scale = jnp.minimum(
        1.0, 0.5 * math.sqrt(CO * 9 * CI) / jnp.sqrt(norm_sq + EPSILON)
    )
    scale = jnp.broadcast_to(clip_scale, (8, 128))[None]
    new_momentum = MOMENTUM_RATE * momentum_ref[...] + scale * combined_ref[...]
    momentum_out[...] = new_momentum
    weight_out[...] = weight_ref[...] - LEARN_RATE * new_momentum


def call_update(terms, combined, weight, momentum):
    return pl.pallas_call(
        update_kernel,
        out_shape=(jax.ShapeDtypeStruct((9, 8, 128), jnp.float32),) * 2,
        in_specs=[VM] * 4,
        out_specs=(VM, VM),
        name="update",
        compiler_params=pltpu.CompilerParams(vmem_limit_bytes=2 * 1024 * 1024),
    )(terms, combined, weight, momentum)


def norm_terms(spread):
    spread = lax.all_to_all(
        spread, ("core", "ch"), 0, 0, tiled=True, axis_index_groups=CROSS_ORDER
    )
    value = jnp.sum(spread, axis=0, keepdims=True)
    spread = jnp.broadcast_to(value, (lax.axis_size(("y", "x")), 1, 128))
    return lax.all_to_all(
        spread, ("y", "x"), 0, 0, tiled=True, axis_index_groups=PLANE_ORDER
    )


def own_rows(value):
    return value.transpose(1, 2, 0, 3).reshape(9, 2, 4, 128).transpose(0, 2, 1, 3).reshape(9, 8, 128)


def whole_rows(value):
    return value.reshape(9, 4, 2, 128).transpose(0, 2, 1, 3).reshape(3, 3, 2, 512).transpose(2, 0, 1, 3)


def local(inputs, grad_out, weight, momentum):
    images, height, across, chan_in = inputs.shape
    chan_out = grad_out.shape[3]
    replicas = lax.axis_size(REP)
    planes = lax.axis_size("ch")
    col_count = chan_in // planes
    own_count = chan_out // replicas
    rep_index = lax.axis_index(REP)
    x_rows = (
        inputs.transpose(1, 2, 0, 3)
        .reshape(AREA, images, 4, 128)
        .transpose(0, 2, 1, 3)
        .reshape(AREA * 8, 128)
    )
    d_rows = grad_out.transpose(1, 2, 0, 3).reshape(AREA * images, chan_out)
    w_rows = weight.transpose(1, 2, 0, 3).reshape(9 * chan_out, chan_in)
    sent = call_grads(x_rows, d_rows).reshape(replicas, 9, 8, 128)
    d_later, sent_held = lax.optimization_barrier((d_rows, sent))
    vectors = lax.all_to_all(
        sent_held, REP, 0, 0, tiled=True, axis_index_groups=REP_ORDER
    )
    parts = call_input(d_later, w_rows)
    total = parts[0]
    for step in (4, 3, 5, 2, 6, 1, 7):
        pairs = [(source, (source + step) % planes) for source in range(planes)]
        total = total + lax.ppermute(parts[step], "ch", pairs)
    input_grad = (
        total
        .reshape(height, across, images, col_count)
        .transpose(2, 0, 1, 3)
    )

    owned_w = lax.dynamic_slice_in_dim(weight, rep_index * own_count, own_count, 0)
    vectors, input_grad, owned_w = lax.optimization_barrier((vectors, input_grad, owned_w))
    combined, spread = call_tree(vectors)
    terms = norm_terms(spread)
    new_weight, new_momentum = call_update(
        terms, combined[0], own_rows(owned_w), own_rows(momentum)
    )
    new_weight, new_momentum = whole_rows(new_weight), whole_rows(new_momentum)
    return (input_grad, new_weight, new_momentum)


def solution(mesh):
    devices = mesh.devices.reshape(8, 4, 2, 8)
    split = jax.sharding.Mesh(devices, REP + ("ch",))
    in_specs = (
        P(REP, None, None, None),
        P(REP, None, None, "ch"),
        P("ch", None, None, None),
        P(("ch",) + REP, None, None, None),
    )
    out_specs = (
        P(REP, None, None, "ch"),
        P(("ch",) + REP, None, None, None),
        P(("ch",) + REP, None, None, None),
    )
    return jax.shard_map(local, mesh=split, in_specs=in_specs, out_specs=out_specs, check_vma=False)
```

```python
import math

import jax
import jax.numpy as jnp
import numpy as np
from jax import lax
from jax.experimental import pallas as pl
from jax.experimental.pallas import tpu as pltpu
from jax.sharding import PartitionSpec as P

CO = 1024
CI = 512
EPSILON = 1e-06
MOMENTUM_RATE = 0.9
LEARN_RATE = 0.05
SIDE = 14
HEAD = 37
REP = ("y", "x", "core")


def chunk_of(replica):
    return {0: HEAD, HEAD: 0}.get(replica, replica)


REP_ORDER = [[chunk_of(place) for place in range(64)]]
CROSS_ORDER = [[(place + 12) % 16 for place in range(16)]]
PLANE_ORDER = [[(place + 18) % 32 for place in range(32)]]
AREA = SIDE * SIDE
TAPS = [(row, col) for row in range(3) for col in range(3)]


def split_bf16(value):
    high = value.astype(jnp.bfloat16)
    low = (value - high.astype(jnp.float32)).astype(jnp.bfloat16)
    return high, low


def lane_masks():
    masks = np.zeros((16, 512), np.float32)
    for tap, (row, col) in enumerate(TAPS):
        for image in range(2):
            for pos in range(AREA):
                high, wide = pos // SIDE - (row - 1), pos % SIDE - (col - 1)
                if 0 <= high < SIDE and 0 <= wide < SIDE:
                    masks[tap, image * 256 + pos] = 1.0
    return masks


def row_masks():
    masks = np.zeros((2, 200, 128), np.float32)
    pos = np.arange(AREA) % SIDE
    masks[0, :AREA] = (pos + 1 < SIDE)[:, None]
    masks[1, :AREA] = (pos - 1 >= 0)[:, None]
    return masks


def grads_kernel(x_hbm, d_hbm, mask_hbm, out_hbm, x_in, d_in, mask_ref, x_hl, d_pad, d_t, lhs, out_a, out_b, out_c, in_sem, out_sem):
    d_copy = pltpu.make_async_copy(d_hbm, d_in, in_sem.at[0])
    x_copy = pltpu.make_async_copy(x_hbm, x_in, in_sem.at[1])
    mask_copy = pltpu.make_async_copy(mask_hbm, mask_ref, in_sem.at[2])
    d_copy.start()
    mask_copy.start()
    x_copy.start()
    d_pad[...] = jnp.zeros_like(d_pad)
    d_copy.wait()
    for image in range(2):
        d_pad[pl.ds(image * 256, AREA), :] = d_in[pl.ds(image, AREA, stride=2), :]
    for part in range(4):
        d_t[part * 128 : (part + 1) * 128, :] = d_pad[part * 128 : (part + 1) * 128, :].T
    halves = []
    for odd in range(2):
        halves.append(
            jnp.concatenate(
                [d_t[pl.ds(part * 128 + odd, 64, stride=2), :] for part in range(4)], axis=1
            )
        )
    base = jnp.concatenate(halves, axis=0)
    mask_copy.wait()

    def fill(taps):
        for tap in taps:
            row, col = TAPS[tap]
            shift = (row - 1) * SIDE + (col - 1)
            moved = base
            if shift:
                moved = jnp.concatenate(
                    [
                        pltpu.roll(base[:, image * 256 : (image + 1) * 256], shift % 256, 1)
                        for image in range(2)
                    ],
                    axis=1,
                )
                moved = moved * mask_ref[tap : tap + 1, :]
            high, low = split_bf16(moved)
            lhs[tap * 128 : (tap + 1) * 128, 0:512] = high
            lhs[tap * 128 : (tap + 1) * 128, 512:1024] = low

    fill(range(0, 3))
    x_copy.wait()
    for image in range(2):
        for block in range(4):
            piece = x_in[pl.ds(block * 2 + image, AREA, stride=8), :]
            piece = jnp.concatenate([piece, jnp.zeros((256 - AREA, 128), jnp.float32)], axis=0)
            high, low = split_bf16(piece)
            cols = slice(block * 128, (block + 1) * 128)
            x_hl[image * 256 : (image + 1) * 256, cols] = high
            x_hl[512 + image * 256 : 512 + (image + 1) * 256, cols] = low
    copies = []
    for group, out in enumerate((out_a, out_b, out_c)):
        if group < 2:
            fill(range(group * 3 + 3, group * 3 + 6))
        rows = slice(group * 384, group * 384 + 384)
        acc = jnp.dot(lhs[rows, 0:256], x_hl[0:256, :], preferred_element_type=jnp.float32)
        acc = acc + jnp.dot(lhs[rows, 512:768], x_hl[0:256, :], preferred_element_type=jnp.float32)
        acc = acc + jnp.dot(lhs[rows, 0:256], x_hl[512:768, :], preferred_element_type=jnp.float32)
        acc = acc + jnp.dot(lhs[rows, 256:512], x_hl[256:512, :], preferred_element_type=jnp.float32)
        acc = acc + jnp.dot(lhs[rows, 768:1024], x_hl[256:512, :], preferred_element_type=jnp.float32)
        acc = acc + jnp.dot(lhs[rows, 256:512], x_hl[768:1024, :], preferred_element_type=jnp.float32)
        for sub in range(3):
            for odd in range(2):
                for block in range(4):
                    out[pl.ds(sub * 8 + block * 2 + odd, 64, stride=24), :] = acc[
                        sub * 128 + odd * 64 : sub * 128 + odd * 64 + 64,
                        block * 128 : (block + 1) * 128,
                    ]
        chunks = out.reshape(64, 24, 128)
        runs = ((0, HEAD, 1), (1, 1, HEAD - 1), (HEAD, 0, 1), (HEAD + 1, HEAD + 1, 63 - HEAD))
        for part, (source, target, count) in enumerate(runs):
            copy = pltpu.make_async_copy(
                chunks.at[pl.ds(source, count)],
                out_hbm.at[pl.ds(target, count), pl.ds(group * 24, 24), :],
                out_sem.at[group * 4 + part],
            )
            copy.start()
            copies.append(copy)
    for copy in copies:
        copy.wait()


VM = pl.BlockSpec(memory_space=pltpu.VMEM)


ANY = pl.BlockSpec(memory_space=pl.ANY)


def call_grads(x_rows, d_rows):
    return pl.pallas_call(
        grads_kernel,
        out_shape=jax.ShapeDtypeStruct((64, 72, 128), jnp.float32),
        in_specs=[ANY, ANY, ANY],
        out_specs=ANY,
        scratch_shapes=[
            pltpu.VMEM((AREA * 8, 128), jnp.float32),
            pltpu.VMEM((AREA * 2, 128), jnp.float32),
            pltpu.VMEM((16, 512), jnp.float32),
            pltpu.VMEM((1024, 512), jnp.bfloat16),
            pltpu.VMEM((512, 128), jnp.float32),
            pltpu.VMEM((512, 128), jnp.float32),
            pltpu.VMEM((1152, 1024), jnp.bfloat16),
            pltpu.VMEM((1536, 128), jnp.float32),
            pltpu.VMEM((1536, 128), jnp.float32),
            pltpu.VMEM((1536, 128), jnp.float32),
            pltpu.SemaphoreType.DMA((3,)),
            pltpu.SemaphoreType.DMA((12,)),
        ],
        name="filter_grads",
        cost_estimate=pl.CostEstimate(
            flops=3 * 2 * 1152 * 512 * 512, bytes_accessed=3500000, transcendentals=0
        ),
    )(x_rows, d_rows, jnp.asarray(lane_masks()))


def input_kernel(d_ref, w_ref, mask_ref, out_ref, d_pad, lhs, w_hl):
    me = lax.axis_index("ch")
    d_pad[...] = jnp.zeros_like(d_pad)
    for image in range(2):
        d_pad[image, 16 : 16 + AREA, :] = d_ref[pl.ds(image, AREA, stride=2), :]
    for tap, (row, col) in enumerate(TAPS):
        shift = (row - 1) * SIDE + (col - 1)
        for image in range(2):
            moved = d_pad[image, 16 - shift : 216 - shift, :]
            if col == 0:
                moved = moved * mask_ref[0]
            if col == 2:
                moved = moved * mask_ref[1]
            high, low = split_bf16(moved)
            rows = slice(image * 208, image * 208 + 200)
            lhs[rows, tap * 128 : (tap + 1) * 128] = high
            lhs[rows, 1152 + tap * 128 : 1152 + (tap + 1) * 128] = low
    high, low = split_bf16(w_ref[...])
    w_hl[0] = high
    w_hl[1] = low
    lane = lax.broadcasted_iota(jnp.int32, (AREA, 128), 1)
    for pair in range(2):
        cols = slice(pair * 256, (pair + 1) * 256)
        acc = jnp.dot(lhs[:, 0:1152], w_hl[0, :, cols], preferred_element_type=jnp.float32)
        acc = acc + jnp.dot(lhs[:, 1152:2304], w_hl[0, :, cols], preferred_element_type=jnp.float32)
        acc = acc + jnp.dot(lhs[:, 0:1152], w_hl[1, :, cols], preferred_element_type=jnp.float32)
        for sub in range(2):
            first = acc[0:AREA, sub * 128 : (sub + 1) * 128]
            second = acc[208 : 208 + AREA, sub * 128 : (sub + 1) * 128]
            dest = pair * 4 + sub * 2
            out_ref[(dest + 8 - me) & 7] = jnp.where(lane < 64, first, pltpu.roll(second, 64, 1))
            out_ref[(dest + 9 - me) & 7] = jnp.where(lane < 64, pltpu.roll(first, 64, 1), second)


def call_input(d_rows, w_rows):
    return pl.pallas_call(
        input_kernel,
        out_shape=jax.ShapeDtypeStruct((8, AREA, 128), jnp.float32),
        in_specs=[VM, VM, VM],
        out_specs=VM,
        scratch_shapes=[
            pltpu.VMEM((2, 240, 128), jnp.float32),
            pltpu.VMEM((416, 2304), jnp.bfloat16),
            pltpu.VMEM((2, 1152, 512), jnp.bfloat16),
        ],
        name="input_grads",
        compiler_params=pltpu.CompilerParams(vmem_limit_bytes=20 * 1024 * 1024),
        cost_estimate=pl.CostEstimate(flops=3 * 2 * 416 * 1152 * 512, bytes_accessed=3500000, transcendentals=0),
    )(d_rows, w_rows, jnp.asarray(row_masks()))


def fold(value):
    value = value + pltpu.roll(value, 4, 1)
    value = value + pltpu.roll(value, 2, 1)
    return jnp.sum(value, axis=2, keepdims=True)


def pair_weights(cross, left_sq, right_sq):
    count = len(cross)
    sums = fold(jnp.stack(cross + left_sq + right_sq, axis=0))
    cross, left_sq, right_sq = sums[:count], sums[count : 2 * count], sums[2 * count :]
    left_w = 1.0 - cross / (2.0 * (left_sq + EPSILON))
    right_w = 1.0 - cross / (2.0 * (right_sq + EPSILON))
    return left_w, right_w


def tree_kernel(v_ref, out_ref, norm_ref, work):
    half = 32
    cross, left_sq, right_sq = [], [], []
    for index in range(half):
        left, right = v_ref[chunk_of(index)], v_ref[chunk_of(index + half)]
        cross.append(jnp.sum(left * right, axis=0))
        left_sq.append(jnp.sum(left * left, axis=0))
        right_sq.append(jnp.sum(right * right, axis=0))
    first = True
    while half > 1:
        left_w, right_w = pair_weights(cross, left_sq, right_sq)
        cross, left_sq, right_sq = [], [], []
        quarter = half // 2
        for index in range(quarter):
            made = []
            for place in (index, index + quarter):
                if first:
                    left, right = v_ref[chunk_of(place)], v_ref[chunk_of(place + half)]
                else:
                    left, right = work[place], work[place + half]
                value = left_w[place] * left + right_w[place] * right
                work[place] = value
                made.append(value)
            left, right = made
            cross.append(jnp.sum(left * right, axis=0))
            left_sq.append(jnp.sum(left * left, axis=0))
            right_sq.append(jnp.sum(right * right, axis=0))
        first = False
        half = quarter
    left_w, right_w = pair_weights(cross, left_sq, right_sq)
    last = left_w[0] * work[0] + right_w[0] * work[1]
    out_ref[0] = last
    norm = jnp.sum(last * last, axis=0)
    norm = jnp.sum(jnp.sum(norm, axis=1, keepdims=True), axis=0, keepdims=True)
    norm_ref[...] = jnp.broadcast_to(norm[None], norm_ref.shape)


def call_tree(vectors):
    return pl.pallas_call(
        tree_kernel,
        out_shape=(
            jax.ShapeDtypeStruct((1, 9, 8, 128), jnp.float32),
            jax.ShapeDtypeStruct((16, 1, 128), jnp.float32),
        ),
        in_specs=[VM],
        out_specs=(VM, VM),
        scratch_shapes=[pltpu.VMEM((32, 9, 8, 128), jnp.float32)],
        name="pair_tree",
        compiler_params=pltpu.CompilerParams(vmem_limit_bytes=10 * 1024 * 1024),
        cost_estimate=pl.CostEstimate(flops=64 * 9216 * 9, bytes_accessed=2400000, transcendentals=0),
    )(vectors)


def update_kernel(terms_ref, combined_ref, weight_ref, momentum_ref, weight_out, momentum_out):
    norm_sq = jnp.sum(terms_ref[...], axis=0)
    clip_scale = jnp.minimum(
        1.0, 0.5 * math.sqrt(CO * 9 * CI) / jnp.sqrt(norm_sq + EPSILON)
    )
    scale = jnp.broadcast_to(clip_scale, (8, 128))[None]
    new_momentum = MOMENTUM_RATE * momentum_ref[...] + scale * combined_ref[...]
    momentum_out[...] = new_momentum
    weight_out[...] = weight_ref[...] - LEARN_RATE * new_momentum


def call_update(terms, combined, weight, momentum):
    return pl.pallas_call(
        update_kernel,
        out_shape=(jax.ShapeDtypeStruct((9, 8, 128), jnp.float32),) * 2,
        in_specs=[VM] * 4,
        out_specs=(VM, VM),
        name="update",
        compiler_params=pltpu.CompilerParams(vmem_limit_bytes=2 * 1024 * 1024),
    )(terms, combined, weight, momentum)


def norm_terms(spread):
    spread = lax.all_to_all(
        spread, ("core", "ch"), 0, 0, tiled=True, axis_index_groups=CROSS_ORDER
    )
    value = jnp.sum(spread, axis=0, keepdims=True)
    spread = jnp.broadcast_to(value, (lax.axis_size(("y", "x")), 1, 128))
    return lax.all_to_all(
        spread, ("y", "x"), 0, 0, tiled=True, axis_index_groups=PLANE_ORDER
    )


def own_rows(value):
    return value.transpose(1, 2, 0, 3).reshape(9, 2, 4, 128).transpose(0, 2, 1, 3).reshape(9, 8, 128)


def whole_rows(value):
    return value.reshape(9, 4, 2, 128).transpose(0, 2, 1, 3).reshape(3, 3, 2, 512).transpose(2, 0, 1, 3)


def local(inputs, grad_out, weight, momentum):
    images, height, across, chan_in = inputs.shape
    chan_out = grad_out.shape[3]
    replicas = lax.axis_size(REP)
    planes = lax.axis_size("ch")
    col_count = chan_in // planes
    own_count = chan_out // replicas
    rep_index = lax.axis_index(REP)
    x_rows = (
        inputs.transpose(1, 2, 0, 3)
        .reshape(AREA, images, 4, 128)
        .transpose(0, 2, 1, 3)
        .reshape(AREA * 8, 128)
    )
    d_rows = grad_out.transpose(1, 2, 0, 3).reshape(AREA * images, chan_out)
    w_rows = weight.transpose(1, 2, 0, 3).reshape(9 * chan_out, chan_in)
    sent = call_grads(x_rows, d_rows).reshape(replicas, 9, 8, 128)
    d_later, sent_held = lax.optimization_barrier((d_rows, sent))
    vectors = lax.all_to_all(
        sent_held, REP, 0, 0, tiled=True, axis_index_groups=REP_ORDER
    )
    parts = call_input(d_later, w_rows)
    total = parts[0]
    for step in (4, 3, 5, 2, 6, 1, 7):
        pairs = [(source, (source + step) % planes) for source in range(planes)]
        total = total + lax.ppermute(parts[step], "ch", pairs)
    input_grad = (
        total
        .reshape(height, across, images, col_count)
        .transpose(2, 0, 1, 3)
    )

    owned_w = lax.dynamic_slice_in_dim(weight, rep_index * own_count, own_count, 0)
    vectors, input_grad, owned_w = lax.optimization_barrier((vectors, input_grad, owned_w))
    combined, spread = call_tree(vectors)
    terms = norm_terms(spread)
    new_weight, new_momentum = call_update(
        terms, combined[0], own_rows(owned_w), own_rows(momentum)
    )
    new_weight, new_momentum = whole_rows(new_weight), whole_rows(new_momentum)
    return (input_grad, new_weight, new_momentum)


def solution(mesh):
    devices = mesh.devices.reshape(8, 4, 2, 8)
    split = jax.sharding.Mesh(devices, REP + ("ch",))
    in_specs = (
        P(REP, None, None, None),
        P(REP, None, None, "ch"),
        P("ch", None, None, None),
        P(("ch",) + REP, None, None, None),
    )
    out_specs = (
        P(REP, None, None, "ch"),
        P(("ch",) + REP, None, None, None),
        P(("ch",) + REP, None, None, None),
    )
    return jax.shard_map(local, mesh=split, in_specs=in_specs, out_specs=out_specs, check_vma=False)
```

```python
import math

import jax
import jax.numpy as jnp
import numpy as np
from jax import lax
from jax.experimental import pallas as pl
from jax.experimental.pallas import tpu as pltpu
from jax.sharding import PartitionSpec as P

CO = 1024
CI = 512
EPSILON = 1e-06
MOMENTUM_RATE = 0.9
LEARN_RATE = 0.05
SIDE = 14
HEAD = 37
REP = ("y", "x", "core")


def chunk_of(replica):
    return {0: HEAD, HEAD: 0}.get(replica, replica)


REP_ORDER = [[chunk_of(place) for place in range(64)]]
CH_ORDER = [[4, 5, 6, 7, 0, 1, 2, 3]]
AREA = SIDE * SIDE
TAPS = [(row, col) for row in range(3) for col in range(3)]


def split_bf16(value):
    high = value.astype(jnp.bfloat16)
    low = (value - high.astype(jnp.float32)).astype(jnp.bfloat16)
    return high, low


def lane_masks():
    masks = np.zeros((16, 512), np.float32)
    for tap, (row, col) in enumerate(TAPS):
        for image in range(2):
            for pos in range(AREA):
                high, wide = pos // SIDE - (row - 1), pos % SIDE - (col - 1)
                if 0 <= high < SIDE and 0 <= wide < SIDE:
                    masks[tap, image * 256 + pos] = 1.0
    return masks


def row_masks():
    masks = np.zeros((2, 200, 128), np.float32)
    pos = np.arange(AREA) % SIDE
    masks[0, :AREA] = (pos + 1 < SIDE)[:, None]
    masks[1, :AREA] = (pos - 1 >= 0)[:, None]
    return masks


def grads_kernel(x_hbm, d_hbm, mask_hbm, out_hbm, x_in, d_in, mask_ref, x_hl, d_pad, d_t, lhs, out_a, out_b, out_c, in_sem, out_sem):
    d_copy = pltpu.make_async_copy(d_hbm, d_in, in_sem.at[0])
    x_copy = pltpu.make_async_copy(x_hbm, x_in, in_sem.at[1])
    mask_copy = pltpu.make_async_copy(mask_hbm, mask_ref, in_sem.at[2])
    d_copy.start()
    mask_copy.start()
    x_copy.start()
    d_pad[...] = jnp.zeros_like(d_pad)
    d_copy.wait()
    for image in range(2):
        d_pad[pl.ds(image * 256, AREA), :] = d_in[pl.ds(image, AREA, stride=2), :]
    for part in range(4):
        d_t[part * 128 : (part + 1) * 128, :] = d_pad[part * 128 : (part + 1) * 128, :].T
    halves = []
    for odd in range(2):
        halves.append(
            jnp.concatenate(
                [d_t[pl.ds(part * 128 + odd, 64, stride=2), :] for part in range(4)], axis=1
            )
        )
    base = jnp.concatenate(halves, axis=0)
    mask_copy.wait()

    def fill(taps):
        for tap in taps:
            row, col = TAPS[tap]
            shift = (row - 1) * SIDE + (col - 1)
            moved = base
            if shift:
                moved = jnp.concatenate(
                    [
                        pltpu.roll(base[:, image * 256 : (image + 1) * 256], shift % 256, 1)
                        for image in range(2)
                    ],
                    axis=1,
                )
                moved = moved * mask_ref[tap : tap + 1, :]
            high, low = split_bf16(moved)
            lhs[tap * 128 : (tap + 1) * 128, 0:512] = high
            lhs[tap * 128 : (tap + 1) * 128, 512:1024] = low

    fill(range(0, 3))
    x_copy.wait()
    for image in range(2):
        for block in range(4):
            piece = x_in[pl.ds(block * 2 + image, AREA, stride=8), :]
            piece = jnp.concatenate([piece, jnp.zeros((256 - AREA, 128), jnp.float32)], axis=0)
            high, low = split_bf16(piece)
            cols = slice(block * 128, (block + 1) * 128)
            x_hl[image * 256 : (image + 1) * 256, cols] = high
            x_hl[512 + image * 256 : 512 + (image + 1) * 256, cols] = low
    copies = []
    for group, out in enumerate((out_a, out_b, out_c)):
        if group < 2:
            fill(range(group * 3 + 3, group * 3 + 6))
        rows = slice(group * 384, group * 384 + 384)
        acc = jnp.dot(lhs[rows, 0:256], x_hl[0:256, :], preferred_element_type=jnp.float32)
        acc = acc + jnp.dot(lhs[rows, 512:768], x_hl[0:256, :], preferred_element_type=jnp.float32)
        acc = acc + jnp.dot(lhs[rows, 0:256], x_hl[512:768, :], preferred_element_type=jnp.float32)
        acc = acc + jnp.dot(lhs[rows, 256:512], x_hl[256:512, :], preferred_element_type=jnp.float32)
        acc = acc + jnp.dot(lhs[rows, 768:1024], x_hl[256:512, :], preferred_element_type=jnp.float32)
        acc = acc + jnp.dot(lhs[rows, 256:512], x_hl[768:1024, :], preferred_element_type=jnp.float32)
        for sub in range(3):
            for odd in range(2):
                for block in range(4):
                    out[pl.ds(sub * 8 + block * 2 + odd, 64, stride=24), :] = acc[
                        sub * 128 + odd * 64 : sub * 128 + odd * 64 + 64,
                        block * 128 : (block + 1) * 128,
                    ]
        chunks = out.reshape(64, 24, 128)
        runs = ((0, HEAD, 1), (1, 1, HEAD - 1), (HEAD, 0, 1), (HEAD + 1, HEAD + 1, 63 - HEAD))
        for part, (source, target, count) in enumerate(runs):
            copy = pltpu.make_async_copy(
                chunks.at[pl.ds(source, count)],
                out_hbm.at[pl.ds(target, count), pl.ds(group * 24, 24), :],
                out_sem.at[group * 4 + part],
            )
            copy.start()
            copies.append(copy)
    for copy in copies:
        copy.wait()


VM = pl.BlockSpec(memory_space=pltpu.VMEM)


ANY = pl.BlockSpec(memory_space=pl.ANY)


def call_grads(x_rows, d_rows):
    return pl.pallas_call(
        grads_kernel,
        out_shape=jax.ShapeDtypeStruct((64, 72, 128), jnp.float32),
        in_specs=[ANY, ANY, ANY],
        out_specs=ANY,
        scratch_shapes=[
            pltpu.VMEM((AREA * 8, 128), jnp.float32),
            pltpu.VMEM((AREA * 2, 128), jnp.float32),
            pltpu.VMEM((16, 512), jnp.float32),
            pltpu.VMEM((1024, 512), jnp.bfloat16),
            pltpu.VMEM((512, 128), jnp.float32),
            pltpu.VMEM((512, 128), jnp.float32),
            pltpu.VMEM((1152, 1024), jnp.bfloat16),
            pltpu.VMEM((1536, 128), jnp.float32),
            pltpu.VMEM((1536, 128), jnp.float32),
            pltpu.VMEM((1536, 128), jnp.float32),
            pltpu.SemaphoreType.DMA((3,)),
            pltpu.SemaphoreType.DMA((12,)),
        ],
        name="filter_grads",
        cost_estimate=pl.CostEstimate(
            flops=3 * 2 * 1152 * 512 * 512, bytes_accessed=3500000, transcendentals=0
        ),
    )(x_rows, d_rows, jnp.asarray(lane_masks()))


def input_kernel(d_ref, w_ref, mask_ref, out_ref, d_pad, lhs, w_hl):
    me = lax.axis_index("ch")
    d_pad[...] = jnp.zeros_like(d_pad)
    for image in range(2):
        d_pad[image, 16 : 16 + AREA, :] = d_ref[pl.ds(image, AREA, stride=2), :]
    for tap, (row, col) in enumerate(TAPS):
        shift = (row - 1) * SIDE + (col - 1)
        for image in range(2):
            moved = d_pad[image, 16 - shift : 216 - shift, :]
            if col == 0:
                moved = moved * mask_ref[0]
            if col == 2:
                moved = moved * mask_ref[1]
            high, low = split_bf16(moved)
            rows = slice(image * 208, image * 208 + 200)
            lhs[rows, tap * 128 : (tap + 1) * 128] = high
            lhs[rows, 1152 + tap * 128 : 1152 + (tap + 1) * 128] = low
    high, low = split_bf16(w_ref[...])
    w_hl[0] = high
    w_hl[1] = low
    lane = lax.broadcasted_iota(jnp.int32, (AREA, 128), 1)
    for pair in range(2):
        cols = slice(pair * 256, (pair + 1) * 256)
        acc = jnp.dot(lhs[:, 0:1152], w_hl[0, :, cols], preferred_element_type=jnp.float32)
        acc = acc + jnp.dot(lhs[:, 1152:2304], w_hl[0, :, cols], preferred_element_type=jnp.float32)
        acc = acc + jnp.dot(lhs[:, 0:1152], w_hl[1, :, cols], preferred_element_type=jnp.float32)
        for sub in range(2):
            first = acc[0:AREA, sub * 128 : (sub + 1) * 128]
            second = acc[208 : 208 + AREA, sub * 128 : (sub + 1) * 128]
            dest = pair * 4 + sub * 2
            out_ref[(dest + 8 - me) & 7] = jnp.where(lane < 64, first, pltpu.roll(second, 64, 1))
            out_ref[(dest + 9 - me) & 7] = jnp.where(lane < 64, pltpu.roll(first, 64, 1), second)


def call_input(d_rows, w_rows):
    return pl.pallas_call(
        input_kernel,
        out_shape=jax.ShapeDtypeStruct((8, AREA, 128), jnp.float32),
        in_specs=[VM, VM, VM],
        out_specs=VM,
        scratch_shapes=[
            pltpu.VMEM((2, 240, 128), jnp.float32),
            pltpu.VMEM((416, 2304), jnp.bfloat16),
            pltpu.VMEM((2, 1152, 512), jnp.bfloat16),
        ],
        name="input_grads",
        compiler_params=pltpu.CompilerParams(vmem_limit_bytes=20 * 1024 * 1024),
        cost_estimate=pl.CostEstimate(flops=3 * 2 * 416 * 1152 * 512, bytes_accessed=3500000, transcendentals=0),
    )(d_rows, w_rows, jnp.asarray(row_masks()))


def fold(value):
    value = value + pltpu.roll(value, 4, 1)
    value = value + pltpu.roll(value, 2, 1)
    return jnp.sum(value, axis=2, keepdims=True)


def pair_weights(cross, left_sq, right_sq):
    count = len(cross)
    sums = fold(jnp.stack(cross + left_sq + right_sq, axis=0))
    cross, left_sq, right_sq = sums[:count], sums[count : 2 * count], sums[2 * count :]
    left_w = 1.0 - cross / (2.0 * (left_sq + EPSILON))
    right_w = 1.0 - cross / (2.0 * (right_sq + EPSILON))
    return left_w, right_w


def tree_kernel(v_ref, out_ref, norm_ref, work):
    half = 32
    cross, left_sq, right_sq = [], [], []
    for index in range(half):
        left, right = v_ref[chunk_of(index)], v_ref[chunk_of(index + half)]
        cross.append(jnp.sum(left * right, axis=0))
        left_sq.append(jnp.sum(left * left, axis=0))
        right_sq.append(jnp.sum(right * right, axis=0))
    first = True
    while half > 1:
        left_w, right_w = pair_weights(cross, left_sq, right_sq)
        cross, left_sq, right_sq = [], [], []
        quarter = half // 2
        for index in range(quarter):
            made = []
            for place in (index, index + quarter):
                if first:
                    left, right = v_ref[chunk_of(place)], v_ref[chunk_of(place + half)]
                else:
                    left, right = work[place], work[place + half]
                value = left_w[place] * left + right_w[place] * right
                work[place] = value
                made.append(value)
            left, right = made
            cross.append(jnp.sum(left * right, axis=0))
            left_sq.append(jnp.sum(left * left, axis=0))
            right_sq.append(jnp.sum(right * right, axis=0))
        first = False
        half = quarter
    left_w, right_w = pair_weights(cross, left_sq, right_sq)
    last = left_w[0] * work[0] + right_w[0] * work[1]
    out_ref[0] = last
    norm = jnp.sum(last * last, axis=0)
    norm = jnp.sum(jnp.sum(norm, axis=1, keepdims=True), axis=0, keepdims=True)
    norm_ref[...] = jnp.broadcast_to(norm[None], norm_ref.shape)


def call_tree(vectors):
    return pl.pallas_call(
        tree_kernel,
        out_shape=(
            jax.ShapeDtypeStruct((1, 9, 8, 128), jnp.float32),
            jax.ShapeDtypeStruct((32, 1, 128), jnp.float32),
        ),
        in_specs=[VM],
        out_specs=(VM, VM),
        scratch_shapes=[pltpu.VMEM((32, 9, 8, 128), jnp.float32)],
        name="pair_tree",
        compiler_params=pltpu.CompilerParams(vmem_limit_bytes=10 * 1024 * 1024),
        cost_estimate=pl.CostEstimate(flops=64 * 9216 * 9, bytes_accessed=2400000, transcendentals=0),
    )(vectors)


def update_kernel(terms_ref, combined_ref, weight_ref, momentum_ref, weight_out, momentum_out):
    norm_sq = jnp.sum(terms_ref[...], axis=0)
    clip_scale = jnp.minimum(
        1.0, 0.5 * math.sqrt(CO * 9 * CI) / jnp.sqrt(norm_sq + EPSILON)
    )
    scale = jnp.broadcast_to(clip_scale, (8, 128))[None]
    new_momentum = MOMENTUM_RATE * momentum_ref[...] + scale * combined_ref[...]
    momentum_out[...] = new_momentum
    weight_out[...] = weight_ref[...] - LEARN_RATE * new_momentum


def call_update(terms, combined, weight, momentum):
    return pl.pallas_call(
        update_kernel,
        out_shape=(jax.ShapeDtypeStruct((9, 8, 128), jnp.float32),) * 2,
        in_specs=[VM] * 4,
        out_specs=(VM, VM),
        name="update",
        compiler_params=pltpu.CompilerParams(vmem_limit_bytes=2 * 1024 * 1024),
    )(terms, combined, weight, momentum)


def norm_terms(spread):
    spread = lax.all_to_all(
        spread, ("y", "x"), 0, 0, tiled=True, axis_index_groups=[[(place + 18) % 32 for place in range(32)]]
    )
    value = jnp.sum(spread, axis=0, keepdims=True)
    spread = jnp.broadcast_to(value, (lax.axis_size(("core", "ch")), 1, 128))
    return lax.all_to_all(
        spread, ("core", "ch"), 0, 0, tiled=True, axis_index_groups=[[(place + 12) % 16 for place in range(16)]]
    )


def own_rows(value):
    return value.transpose(1, 2, 0, 3).reshape(9, 2, 4, 128).transpose(0, 2, 1, 3).reshape(9, 8, 128)


def whole_rows(value):
    return value.reshape(9, 4, 2, 128).transpose(0, 2, 1, 3).reshape(3, 3, 2, 512).transpose(2, 0, 1, 3)


def local(inputs, grad_out, weight, momentum):
    images, height, across, chan_in = inputs.shape
    chan_out = grad_out.shape[3]
    replicas = lax.axis_size(REP)
    planes = lax.axis_size("ch")
    col_count = chan_in // planes
    own_count = chan_out // replicas
    rep_index = lax.axis_index(REP)
    x_rows = (
        inputs.transpose(1, 2, 0, 3)
        .reshape(AREA, images, 4, 128)
        .transpose(0, 2, 1, 3)
        .reshape(AREA * 8, 128)
    )
    d_rows = grad_out.transpose(1, 2, 0, 3).reshape(AREA * images, chan_out)
    w_rows = weight.transpose(1, 2, 0, 3).reshape(9 * chan_out, chan_in)
    sent = call_grads(x_rows, d_rows).reshape(replicas, 9, 8, 128)
    d_later, sent_held = lax.optimization_barrier((d_rows, sent))
    vectors = lax.all_to_all(
        sent_held, REP, 0, 0, tiled=True, axis_index_groups=REP_ORDER
    )
    parts = call_input(d_later, w_rows)
    total = parts[0]
    for step in (4, 3, 5, 2, 6, 1, 7):
        pairs = [(source, (source + step) % planes) for source in range(planes)]
        total = total + lax.ppermute(parts[step], "ch", pairs)
    input_grad = (
        total
        .reshape(height, across, images, col_count)
        .transpose(2, 0, 1, 3)
    )

    owned_w = lax.dynamic_slice_in_dim(weight, rep_index * own_count, own_count, 0)
    vectors, input_grad, owned_w = lax.optimization_barrier((vectors, input_grad, owned_w))
    combined, spread = call_tree(vectors)
    terms = norm_terms(spread)
    new_weight, new_momentum = call_update(
        terms, combined[0], own_rows(owned_w), own_rows(momentum)
    )
    new_weight, new_momentum = whole_rows(new_weight), whole_rows(new_momentum)
    return (input_grad, new_weight, new_momentum)


def solution(mesh):
    devices = mesh.devices.reshape(8, 4, 2, 8)
    split = jax.sharding.Mesh(devices, REP + ("ch",))
    in_specs = (
        P(REP, None, None, None),
        P(REP, None, None, "ch"),
        P("ch", None, None, None),
        P(("ch",) + REP, None, None, None),
    )
    out_specs = (
        P(REP, None, None, "ch"),
        P(("ch",) + REP, None, None, None),
        P(("ch",) + REP, None, None, None),
    )
    return jax.shard_map(local, mesh=split, in_specs=in_specs, out_specs=out_specs, check_vma=False)
```
